32 devices in a mesh: ctx: 8 (over y, x, core), tp: 4 (over z).
Axes of the slice: x: 2, y: 2, z: 4, core: 2. Of those that a mesh axis runs over, the one named last changes fastest.
Arguments:
- queries: bfloat16 [2048, 4096], P('ctx', 'tp'), may hold values from -100 to 100
- key_pages: bfloat16 [32, 64, 1024], P('ctx', None, 'tp'), may hold values from -5 to 5
- value_pages: bfloat16 [32, 64, 1024], P('ctx', None, 'tp'), may hold values from -6 to 6
- mixer_input: bfloat16 [2048, 4096], P('ctx', 'tp'), may hold values from -6 to 6
- state_write: bfloat16 [2048, 1024], P('ctx', 'tp'), may hold values from -0.029907227 to 0.029907227
- state_read: bfloat16 [2048, 1024], P('ctx', 'tp'), may hold values from -6 to 6
- log_decay: float32 [32, 2048], P('tp', 'ctx'), may hold values from -1 to 0
- skip_gain: float32 [32], P('tp'), may hold values from 0.5 to 1.5
- doc_lengths: int32 [4], replicated, may hold values from 1 to 1024, 2048 in all
- page_table: int32 [32], replicated, may hold values from 0 to 31, as said below
- attention_weight: bfloat16 [4096, 4096], P('tp'), may hold values from -0.75 to 0.75
- mixer_weight: bfloat16 [4096, 4096], P('tp'), may hold values from -0.09375 to 0.09375
Outputs:
- mixed: bfloat16 [2048, 4096], P(('ctx', 'tp'))
The draws below stay inside these ranges and needn't reach their ends.
Inputs may be any that keep to these rules, and one draw needn't show every extreme that they name: `doc_lengths`: the lengths sum to 2048; the longest is exactly 1024. `page_table`: A permutation: every physical page holds exactly one logical page.
All inputs are finite; a program needn't handle non-finite values.
Results may differ from the reference program's by a relative error of at most 0.007.
Values may be sent and summed in bfloat16 or wider, within the bound.
No kernel may reach another device: no remote copies, remote signals or barrier semaphores. Data moves between devices by JAX's collectives and lax.ppermute only.
A program may use at most 256 MiB of HBM per device.

```python
import math
import jax
import jax.numpy as jnp
import numpy as np
from jax import lax

D = 4096
HEADS = 32
KV_HEADS = 8
HEAD_DIM = 128
SSM_HEADS = 32
SSM_HEAD_DIM = 128
STATE = 128
GROUPS = 8
PAGE = 64
DOCS = 4
TOK_DEV = 256
PACKED_TOKENS = 2048
PAGES = 32
LONGEST = 1024
N_CTX = 8


def page_order(key):
    return jax.random.permutation(jax.random.fold_in(key, 7), PAGES).astype(jnp.int32)


def final_keys(key):
    row_width = KV_HEADS * HEAD_DIM
    base_key = jax.random.fold_in(key, 3)
    key_rows = jnp.clip(jax.random.normal(base_key, (PACKED_TOKENS, row_width), jnp.float32), -5.0, 5.0)
    return key_rows


def draw_page_table(key, part):
    return page_order(key)


def draw_key_pages(key, part):
    key_rows = final_keys(key)
    page_rows = key_rows.reshape(PAGES, PAGE, KV_HEADS * HEAD_DIM)
    physical = jnp.zeros_like(page_rows).at[page_order(key)].set(page_rows)
    return physical.astype(jnp.bfloat16)


def draw_queries(key, part):
    query_key = jax.random.fold_in(key, 4)
    row_width = HEADS * HEAD_DIM
    base = jnp.clip(1.5 * jax.random.normal(query_key, (PACKED_TOKENS, row_width), jnp.float32), -9.0, 9.0)
    return base.astype(jnp.bfloat16)


def draw_log_decay(key, part):
    fast_share = 0.5
    fast_heads = jax.random.bernoulli(jax.random.fold_in(key, 21), fast_share, (SSM_HEADS,))
    fast_rate = jnp.exp(jax.random.uniform(jax.random.fold_in(key, 22), (SSM_HEADS,), jnp.float32, math.log(0.02), math.log(0.03)))
    slow_rate = jnp.exp(jax.random.uniform(jax.random.fold_in(key, 23), (SSM_HEADS,), jnp.float32, math.log(0.1 / PACKED_TOKENS), math.log(0.5 / PACKED_TOKENS)))
    head_fraction = jnp.where(fast_heads, fast_rate, slow_rate)
    token_multiplier = jax.random.uniform(jax.random.fold_in(key, 24), (SSM_HEADS, PACKED_TOKENS), jnp.float32, 0.5, 2.0)
    block_multiplier = jnp.exp(jax.random.uniform(jax.random.fold_in(key, 25), (SSM_HEADS, PACKED_TOKENS // TOK_DEV), jnp.float32, math.log(0.5), math.log(2.0)))
    block_multiplier = jnp.repeat(block_multiplier, TOK_DEV, axis=1)
    spike_position = jax.random.randint(jax.random.fold_in(key, 26), (3,), 0, PACKED_TOKENS)
    spike_length = jax.random.uniform(jax.random.fold_in(key, 27), (3,), jnp.float32, 0.22, 0.69)
    spike_penalty = jnp.zeros((PACKED_TOKENS,), jnp.float32).at[spike_position].add(spike_length)
    return -(head_fraction[:, None] * token_multiplier * block_multiplier) - spike_penalty[None, :]


def level_of(key, dims, shards, low, high):
    def one(position, shards_of):
        steps = jax.random.uniform(jax.random.fold_in(jax.random.fold_in(key, 6), position), (shards_of,), jnp.float32, low / len(shards), high / len(shards))
        return jnp.repeat(jnp.exp(steps), dims[position] // shards_of).reshape((-1,) + (1,) * (len(dims) - position - 1))

    gain = one(*shards[0])
    for cut in shards[1:]:
        gain = gain * one(*cut)
    return gain


def length_profile(count, total, most, skew):
    loads = [(1 << 20) // math.isqrt(grade ** skew) + 1 for grade in range(2, count + 1)]
    surplus, counts = total - most - (count - 1), [1] * (count - 1)
    while surplus > 0:
        free = [i for i in range(count - 1) if counts[i] < most]
        whole, left = sum([loads[i] for i in free]), surplus
        for i in free:
            addition = min(most - counts[i], max(1, left * loads[i] // whole), surplus)
            counts[i] = counts[i] + addition
            surplus = surplus - addition
    return np.array([most] + counts)


def ragged_sizes(own_key, amount, total, most, skew):
    if amount == 2:
        one = jax.random.randint(own_key, (), max(1, total - most), min(most, total - 1) + 1)
        return jnp.stack([one, total - one])
    sizes = jnp.asarray(length_profile(amount, total, most, skew), jnp.int32)
    pairs = (amount - 1) // 2
    donor, sink = sizes[1:1 + 2 * pairs:2], sizes[2:2 + 2 * pairs:2]
    room = jnp.minimum(donor - 1, most - sink)
    passed = jax.random.randint(jax.random.fold_in(own_key, 1), (pairs,), 0, 1 << 20) % (room + 1)
    sizes = sizes.at[1:1 + 2 * pairs:2].set(donor - passed).at[2:2 + 2 * pairs:2].set(sink + passed)
    return sizes[jax.random.permutation(jax.random.fold_in(own_key, 2), amount)]


def normal_values(rng, shape, deviation, most, pieces=(), kind=jnp.bfloat16):
    result = jax.random.normal(rng, shape, jnp.float32) * deviation
    if len(pieces) > 0:
        result = level_of(rng, shape, pieces, -0.22, 0.18) * result
    return jnp.clip(result, min=-most, max=most).astype(kind)


def setup_inputs(seed: int = 0) -> dict:
    key_of = jax.random.split(jax.random.key(seed), 13)
    queries = draw_queries(jax.random.fold_in(key_of[12], 71), 0)
    key_pages = draw_key_pages(jax.random.fold_in(key_of[12], 71), 0)
    value_pages = normal_values(key_of[2], (PAGES, PAGE, KV_HEADS * HEAD_DIM), 1.0, 6.0, ((0, 8), (2, 4)))
    mixer_input = normal_values(key_of[3], (PACKED_TOKENS, SSM_HEADS * SSM_HEAD_DIM), 1.0, 6.0, ((0, 8), (1, 4)))
    state_write = normal_values(key_of[4], (PACKED_TOKENS, GROUPS * STATE), 0.005, 0.029907227, ((0, 8), (1, 4)))
    state_read = normal_values(key_of[5], (PACKED_TOKENS, GROUPS * STATE), 1.0, 6.0, ((0, 8), (1, 4)))
    log_decay = draw_log_decay(jax.random.fold_in(key_of[12], 71), 0)
    skip_gain = jnp.clip(0.5 + 1.0 * jax.random.uniform(key_of[7], (SSM_HEADS,), jnp.float32) ** level_of(key_of[7], (SSM_HEADS,), ((0, 4),), -0.2, 0.2), 0.5, 1.5)
    doc_lengths = ragged_sizes(key_of[8], DOCS, PACKED_TOKENS, LONGEST, 2).astype(jnp.int32)
    page_table = draw_page_table(jax.random.fold_in(key_of[12], 71), 0)
    attention_weight = normal_values(key_of[10], (HEADS * HEAD_DIM, D), (HEADS * HEAD_DIM // 64) ** -0.5, 0.75, ((0, 4),))
    mixer_weight = normal_values(key_of[11], (SSM_HEADS * SSM_HEAD_DIM, D), (SSM_HEADS * SSM_HEAD_DIM) ** -0.5, 0.09375, ((0, 4),))
    return dict(queries=queries, key_pages=key_pages, value_pages=value_pages, mixer_input=mixer_input, state_write=state_write, state_read=state_read, log_decay=log_decay, skip_gain=skip_gain, doc_lengths=doc_lengths, page_table=page_table, attention_weight=attention_weight, mixer_weight=mixer_weight)


def segment_ids(positions, doc_ends):
    return jnp.sum((positions[:, None] >= doc_ends[None, :]).astype(jnp.int32), axis=1).astype(jnp.int32)


def mixer_local(head_input, write_rows, read_rows, decay_rows, block_seg, prev_seg, per_group):
    tok_rows = head_input.shape[0]
    decay_sum = jnp.cumsum(decay_rows, axis=1)
    token_order = jnp.arange(tok_rows, dtype=jnp.int32)
    visible = (token_order[None, :] <= token_order[:, None]) & (block_seg[None, :] == block_seg[:, None])
    decay_diff = decay_sum[:, :, None] - decay_sum[:, None, :]
    decay_mat = jnp.where(visible[None], jnp.exp(jnp.minimum(decay_diff, 0.0)), 0.0)
    inner_prod = jnp.einsum("tgn,sgn->gts", read_rows.astype(jnp.float32), write_rows.astype(jnp.float32))
    mixing = (decay_mat * jnp.repeat(inner_prod, per_group, axis=0)).astype(jnp.bfloat16)
    intra_out = jnp.einsum("hts,shp->thp", mixing.astype(jnp.float32), head_input.astype(jnp.float32))
    end_seg = block_seg[-1]
    end_weight = jnp.where((block_seg == end_seg)[None, :], jnp.exp(decay_sum[:, -1:] - decay_sum), 0.0)
    write_heads = jnp.repeat(write_rows, per_group, axis=1).astype(jnp.float32)
    end_write = (jnp.transpose(end_weight)[:, :, None] * write_heads).astype(jnp.bfloat16)
    block_state = jnp.einsum("thn,thp->hnp", end_write.astype(jnp.float32), head_input.astype(jnp.float32))
    block_gain = jnp.where(end_seg == prev_seg, jnp.exp(decay_sum[:, -1]), 0.0)
    return intra_out, block_gain, block_state, decay_sum


def mixer_entry(intra_out, decay_sum, read_rows, head_input, skip_gain, block_seg, prev_seg, state_in, per_group):
    read_heads = jnp.repeat(read_rows, per_group, axis=1).astype(jnp.float32)
    inter_out = jnp.einsum("thn,hnp->thp", read_heads, state_in, precision=lax.Precision.HIGHEST)
    entry_gain = jnp.where((block_seg == prev_seg)[None, :], jnp.exp(decay_sum), 0.0)
    return intra_out + jnp.transpose(entry_gain)[:, :, None] * inter_out + skip_gain[None, :, None] * head_input.astype(jnp.float32)


def reference(queries, key_pages, value_pages, mixer_input, state_write, state_read, log_decay, skip_gain, doc_lengths, page_table, attention_weight, mixer_weight):
    doc_ends = jnp.cumsum(doc_lengths).astype(jnp.int32)
    positions = jnp.arange(PACKED_TOKENS, dtype=jnp.int32)
    seg = segment_ids(positions, doc_ends)
    key_logical = key_pages[page_table].reshape(PACKED_TOKENS, KV_HEADS, HEAD_DIM)
    value_logical = value_pages[page_table].reshape(PACKED_TOKENS, KV_HEADS, HEAD_DIM)
    query_heads = queries.reshape(PACKED_TOKENS, HEADS, HEAD_DIM)
    query_block = math.gcd(PACKED_TOKENS, 1024)
    block_count = PACKED_TOKENS // query_block
    group_size = HEADS // KV_HEADS

    def one_head(head_index):
        kv_index = (head_index // group_size).astype(jnp.int32)
        key_head = lax.dynamic_index_in_dim(key_logical, kv_index, 1, False)
        value_head = lax.dynamic_index_in_dim(value_logical, kv_index, 1, False)
        query_head = lax.dynamic_index_in_dim(query_heads, head_index.astype(jnp.int32), 1, False)

        def one_block(block_index):
            begin_row = (block_index * query_block).astype(jnp.int32)
            query_rows = lax.dynamic_slice_in_dim(query_head, begin_row, query_block)
            query_pos = begin_row + jnp.arange(query_block, dtype=jnp.int32)
            query_seg = lax.dynamic_slice_in_dim(seg, begin_row, query_block)
            scores = jnp.dot(query_rows, key_head.T, preferred_element_type=jnp.float32) * (HEAD_DIM ** -0.5)
            visible = (positions[None, :] <= query_pos[:, None]) & (seg[None, :] == query_seg[:, None])
            row_max = jnp.max(jnp.where(visible, scores, -1e30), axis=1)
            weights = jnp.where(visible, jnp.exp(scores - row_max[:, None]), 0.0)
            probabilities = weights.astype(jnp.bfloat16)
            return jnp.dot(probabilities, value_head, preferred_element_type=jnp.float32) / jnp.sum(weights, axis=1)[:, None]

        return lax.map(one_block, jnp.arange(block_count, dtype=jnp.int32)).reshape(PACKED_TOKENS, HEAD_DIM)

    head_outputs = lax.map(one_head, jnp.arange(HEADS, dtype=jnp.int32))
    attention_out = jnp.transpose(head_outputs, (1, 0, 2)).reshape(PACKED_TOKENS, HEADS * HEAD_DIM).astype(jnp.bfloat16)

    per_group = SSM_HEADS // GROUPS
    block_inputs = mixer_input.reshape(N_CTX, TOK_DEV, SSM_HEADS, SSM_HEAD_DIM)
    block_writes = state_write.reshape(N_CTX, TOK_DEV, GROUPS, STATE)
    block_reads = state_read.reshape(N_CTX, TOK_DEV, GROUPS, STATE)
    block_decays = jnp.transpose(log_decay.reshape(SSM_HEADS, N_CTX, TOK_DEV), (1, 0, 2))
    block_segs = seg.reshape(N_CTX, TOK_DEV)
    prev_segs = jnp.concatenate([jnp.full((1,), -1, jnp.int32), block_segs[:-1, -1]]).astype(jnp.int32)

    def advance(state_in, inputs):
        head_input, write_rows, read_rows, decay_rows, block_seg, prev_seg = inputs
        intra_out, block_gain, block_state, decay_sum = mixer_local(head_input, write_rows, read_rows, decay_rows, block_seg, prev_seg, per_group)
        output = mixer_entry(intra_out, decay_sum, read_rows, head_input, skip_gain, block_seg, prev_seg, state_in, per_group)
        return block_gain[:, None, None] * state_in + block_state, output

    initial = jnp.zeros((SSM_HEADS, STATE, SSM_HEAD_DIM), jnp.float32)
    final_state, mixer_blocks = lax.scan(advance, initial, (block_inputs, block_writes, block_reads, block_decays, block_segs, prev_segs))
    mixer_out = mixer_blocks.reshape(PACKED_TOKENS, SSM_HEADS * SSM_HEAD_DIM).astype(jnp.bfloat16)
    total = jnp.dot(attention_out, attention_weight, preferred_element_type=jnp.float32) + jnp.dot(mixer_out, mixer_weight, preferred_element_type=jnp.float32)
    return total.astype(jnp.bfloat16)
```

```python
import functools

import jax
import jax.numpy as jnp
from jax import lax
from jax.experimental import pallas as pl
from jax.experimental.pallas import tpu as pltpu
from jax.sharding import PartitionSpec as P

HEAD_DIM = 128
SSM_HEAD_DIM = 128
STATE = 128
LOG2E = 1.4426950408889634
LOW = -1e30
F32 = jnp.float32
BF16 = jnp.bfloat16

VMEM_SPEC = pl.BlockSpec(memory_space=pltpu.VMEM)
SMEM_SPEC = pl.BlockSpec(memory_space=pltpu.SMEM)


def doc_ends_of(len_ref):
    ends, total = [], 0
    for i in range(len_ref.shape[0]):
        total = total + len_ref[i]
        ends.append(total)
    return ends


def doc_start(pos, ends):
    start = jnp.zeros_like(pos)
    for end in ends:
        start = jnp.where(pos >= end, end, start)
    return start


def row_slot(part, z):
    d = part ^ z
    return jnp.where(d == 1, 0, jnp.where(d == 3, 1, jnp.where(d == 0, 2, 3)))


def nt(a, b):
    return lax.dot_general(a, b, (((1,), (1,)), ((), ())), preferred_element_type=F32)


def nn(a, b):
    return lax.dot_general(a, b, (((1,), (0,)), ((), ())), preferred_element_type=F32)


def mixer_kernel(len_ref, skip_ref, x_ref, w_ref, r_ref, ld_ref, base_ref, st_ref, eg_ref):
    me = lax.axis_index("ctx")
    heads, rows = ld_ref.shape
    groups = w_ref.shape[1] // STATE
    per_group = heads // groups
    half = heads // 2
    first = me * rows
    ends = doc_ends_of(len_ref)
    ds = ld_ref[...]
    lane = lax.broadcasted_iota(jnp.int32, ds.shape, 1)
    shift = 1
    while shift < rows:
        ds = ds + jnp.where(lane >= shift, pltpu.roll(ds, shift, 1), 0.0)
        shift *= 2
    col = ds.T
    t_pos = first + lax.broadcasted_iota(jnp.int32, (rows, 1), 0)
    t_start = doc_start(t_pos, ends)
    s_pos = first + lax.broadcasted_iota(jnp.int32, (1, rows), 1)
    last = first + rows - 1
    last_start = doc_start(jnp.full((1, 1), last, jnp.int32), ends)
    visible = (s_pos <= t_pos) & (s_pos >= t_start)
    bias = jnp.where(visible, 0.0, LOW)
    eg_ref[...] = jnp.where(t_start < first, jnp.exp(col), 0.0)
    total = ds[:, rows - 1 : rows]
    end_weight = jnp.where(s_pos >= last_start, jnp.exp(total - ds), 0.0)
    gain = jnp.where(last_start < first, jnp.exp(total), 0.0)
    gain = jnp.broadcast_to(gain, (heads, SSM_HEAD_DIM)).astype(BF16)
    pad = jnp.zeros((st_ref.shape[1] - half * STATE - half, SSM_HEAD_DIM), BF16)
    for c in range(2):
        st_ref[c, half * STATE :, :] = jnp.concatenate(
            [gain[c * half : (c + 1) * half].astype(F32), pad.astype(F32)], axis=0
        ).astype(BF16)
    for g in range(groups):
        cols = slice(g * STATE, (g + 1) * STATE)
        write, read = w_ref[:, cols], r_ref[:, cols]
        inner = nt(read, write)
        write_t = write.astype(F32).T
        for h in range(g * per_group, (g + 1) * per_group):
            hc = slice(h * SSM_HEAD_DIM, (h + 1) * SSM_HEAD_DIM)
            x = x_ref[:, hc]
            decay = jnp.exp((col[:, h : h + 1] - ds[h : h + 1, :]) + bias)
            mixing = (decay * inner).astype(BF16)
            base_ref[:, hc] = nn(mixing, x) + skip_ref[h] * x.astype(F32)
            end_write = (write_t * end_weight[h : h + 1, :]).astype(BF16)
            c, i = divmod(h, half)
            st_ref[c, i * STATE : (i + 1) * STATE, :] = nn(end_write, x).astype(BF16)


def mixer_local(doc_lengths, skip_gain, x, w, r, ld):
    heads, rows = ld.shape
    half = heads // 2
    return pl.pallas_call(
        mixer_kernel,
        out_shape=(
            jax.ShapeDtypeStruct(x.shape, F32),
            jax.ShapeDtypeStruct((2, half * STATE + 16, SSM_HEAD_DIM), BF16),
            jax.ShapeDtypeStruct((rows, heads), F32),
        ),
        in_specs=[SMEM_SPEC, SMEM_SPEC] + [VMEM_SPEC] * 4,
        out_specs=(VMEM_SPEC,) * 3,
        compiler_params=pltpu.CompilerParams(vmem_limit_bytes=24 << 20),
        cost_estimate=pl.CostEstimate(
            flops=2 * heads * rows * rows * 128 * 2,
            bytes_accessed=4 << 20,
            transcendentals=heads * rows * rows,
        ),
        name="mixer_local",
    )(doc_lengths, skip_gain, x, w, r, ld)


def compose_kernel(mine_ref, other_ref, out_ref):
    core = lax.axis_index("ctx") & 1
    state_rows = out_ref.shape[0] - 16
    half = state_rows // STATE
    a, b = mine_ref[core].astype(F32), other_ref[core].astype(F32)
    first = jnp.where(core == 0, a, b)
    second = jnp.where(core == 0, b, a)
    for i in range(half):
        rows = slice(i * STATE, (i + 1) * STATE)
        gain = second[state_rows + i : state_rows + i + 1]
        out_ref[rows, :] = (gain * first[rows] + second[rows]).astype(BF16)
    out_ref[state_rows:, :] = (first[state_rows:] * second[state_rows:]).astype(BF16)


def compose(mine, other):
    return pl.pallas_call(
        compose_kernel,
        out_shape=jax.ShapeDtypeStruct(mine.shape[1:], BF16),
        in_specs=[VMEM_SPEC] * 2,
        out_specs=VMEM_SPEC,
        cost_estimate=pl.CostEstimate(flops=1 << 17, bytes_accessed=1 << 20, transcendentals=0),
        name="compose",
    )(mine, other)


def carry_kernel(*refs):
    *got, out_ref, held = refs
    chip = lax.axis_index("ctx") // 2
    for j, ref in enumerate(got, 1):
        held[chip ^ j] = ref[...]
    state_rows = out_ref.shape[0]
    half = state_rows // STATE
    out_ref[...] = jnp.zeros_like(out_ref)

    def one(k, carry):
        gains = held[k, state_rows:, :].astype(F32)
        new = []
        for i in range(half):
            term = held[k, i * STATE : (i + 1) * STATE, :].astype(F32)
            new.append(gains[i : i + 1] * carry[i] + term)
        return tuple(new)

    zero = tuple(jnp.zeros((STATE, SSM_HEAD_DIM), F32) for _ in range(half))
    carry = lax.fori_loop(0, chip, one, zero)
    for i in range(half):
        out_ref[i * STATE : (i + 1) * STATE, :] = carry[i].astype(BF16)


def carry_in(got):
    rows = got[0].shape[0]
    return pl.pallas_call(
        carry_kernel,
        out_shape=jax.ShapeDtypeStruct((rows - 16, SSM_HEAD_DIM), BF16),
        in_specs=[VMEM_SPEC] * len(got),
        out_specs=VMEM_SPEC,
        scratch_shapes=[pltpu.VMEM((len(got) + 1, rows, SSM_HEAD_DIM), BF16)],
        cost_estimate=pl.CostEstimate(flops=1 << 18, bytes_accessed=1 << 20, transcendentals=0),
        name="carry_in",
    )(*got)


def finish_kernel(base_ref, r_ref, eg_ref, mine_ref, other_ref, st_ref, out_ref):
    core = lax.axis_index("ctx") & 1
    z = lax.axis_index("tp")
    rows = base_ref.shape[0]
    part = rows // 4
    half = mine_ref.shape[0] // STATE
    groups = r_ref.shape[1] // STATE
    heads = 2 * half
    per_group = heads // groups
    state_rows = half * STATE
    for h in range(heads):
        c, i = divmod(h, half)
        g = h // per_group
        hs = slice(i * STATE, (i + 1) * STATE)
        a, b = mine_ref[hs, :].astype(F32), other_ref[hs, :].astype(F32)
        entering = jnp.where(core == c, a, b)
        prev = st_ref[c, hs, :].astype(F32)
        gain = st_ref[c, state_rows + i : state_rows + i + 1, :].astype(F32)
        carry = jnp.where(core == 1, gain * entering + prev, entering).astype(BF16)
        hc = slice(h * SSM_HEAD_DIM, (h + 1) * SSM_HEAD_DIM)
        inter = nn(r_ref[:, g * STATE : (g + 1) * STATE], carry)
        res = (base_ref[:, hc] + eg_ref[:, h : h + 1] * inter).astype(BF16)
        for q in range(4):
            at = pl.multiple_of(row_slot(q, z) * part, part)
            out_ref[pl.ds(at, part), hc] = res[q * part : (q + 1) * part]


def finish(base, r, eg, mine, other, st_other):
    return pl.pallas_call(
        finish_kernel,
        out_shape=jax.ShapeDtypeStruct(base.shape, BF16),
        in_specs=[VMEM_SPEC] * 6,
        out_specs=VMEM_SPEC,
        cost_estimate=pl.CostEstimate(
            flops=2 * base.size * STATE, bytes_accessed=2 << 20, transcendentals=0
        ),
        name="finish",
    )(base, r, eg, mine, other, st_other)


def attention_kernel(page_len, len_ref, table_ref, q_ref, *refs):
    *got, out_ref, inv, ks, vs, sc, mx, ls, acc = refs
    me = lax.axis_index("ctx")
    z = lax.axis_index("tp")
    rows = q_ref.shape[0]
    part = rows // 4
    heads = q_ref.shape[1] // HEAD_DIM
    kv_heads = ks.shape[1] // HEAD_DIM
    group = heads // kv_heads
    first = me * rows
    ends = doc_ends_of(len_ref)
    start0 = 0
    for end in ends:
        start0 = jnp.where(first >= end, end, start0)
    low_block = start0 // rows
    pages_block = rows // page_len

    def invert(l, _):
        inv[table_ref[l]] = l
        return 0

    lax.fori_loop(0, table_ref.shape[0], invert, 0)
    low_page, high_page = low_block * pages_block, (me + 1) * pages_block
    for j, ref in enumerate(got):
        for slot in range(ref.shape[1] // page_len):
            page = inv[(me ^ j) * (ref.shape[1] // page_len) + slot]

            @pl.when((page >= low_page) & (page < high_page))
            def _():
                at = pl.ds(pl.multiple_of(page * page_len, page_len), page_len)
                here = slice(slot * page_len, (slot + 1) * page_len)
                ks[at, :] = ref[0, here, :]
                vs[at, :] = ref[1, here, :]

    t_pos = first + lax.broadcasted_iota(jnp.int32, (rows, 1), 0)
    t_start = doc_start(t_pos, ends)
    scale = LOG2E * HEAD_DIM ** (-0.5)

    def scores(block, own):
        at = pl.ds(pl.multiple_of(block * rows, rows), rows)
        u_pos = block * rows + lax.broadcasted_iota(jnp.int32, (1, rows), 1)
        shown = u_pos >= t_start
        if own:
            shown = shown & (u_pos <= t_pos)
        for h in range(heads):
            g = h // group
            s = nt(
                q_ref[:, h * HEAD_DIM : (h + 1) * HEAD_DIM],
                ks[at, g * HEAD_DIM : (g + 1) * HEAD_DIM],
            )
            s = jnp.where(shown, s * scale, LOW)
            sc[block - low_block, h] = s
            top = s[:, :128]
            for k in range(128, rows, 128):
                top = jnp.maximum(top, s[:, k : k + 128])
            mx[h] = top if own else jnp.maximum(mx[h], top)

    scores(me, True)

    def earlier(block, _):
        scores(block, False)
        return 0

    lax.fori_loop(low_block, me, earlier, 0)
    for h in range(heads):
        mx[h] = jnp.broadcast_to(jnp.max(mx[h], axis=1, keepdims=True), (rows, 128))
    ls[...] = jnp.zeros_like(ls)
    acc[...] = jnp.zeros_like(acc)

    def weigh(block, _):
        at = pl.ds(pl.multiple_of(block * rows, rows), rows)
        for h in range(heads):
            g = h // group
            m = mx[h]
            total = ls[h]
            pieces = []
            for k in range(0, rows, 128):
                w = jnp.exp2(sc[block - low_block, h, :, k : k + 128] - m)
                total = total + w
                pieces.append(w.astype(BF16))
            ls[h] = total
            acc[h] += nn(
                jnp.concatenate(pieces, axis=1), vs[at, g * HEAD_DIM : (g + 1) * HEAD_DIM]
            )
        return 0

    lax.fori_loop(low_block, me + 1, weigh, 0)
    for h in range(heads):
        res = (acc[h] / jnp.sum(ls[h], axis=1, keepdims=True)).astype(BF16)
        for q in range(4):
            at = pl.multiple_of(row_slot(q, z) * part, part)
            out_ref[pl.ds(at, part), h * HEAD_DIM : (h + 1) * HEAD_DIM] = res[
                q * part : (q + 1) * part
            ]


def attention(page_len, doc_lengths, page_table, queries, got):
    rows = queries.shape[0]
    heads = queries.shape[1] // HEAD_DIM
    keys = len(got) * got[0].shape[1]
    width = got[0].shape[2]
    blocks = min(keys // rows, keys // 2 // rows + 1)
    return pl.pallas_call(
        functools.partial(attention_kernel, page_len),
        out_shape=jax.ShapeDtypeStruct(queries.shape, BF16),
        in_specs=[SMEM_SPEC, SMEM_SPEC, VMEM_SPEC] + [VMEM_SPEC] * len(got),
        out_specs=VMEM_SPEC,
        scratch_shapes=[
            pltpu.SMEM((page_table.shape[0],), jnp.int32),
            pltpu.VMEM((keys, width), BF16),
            pltpu.VMEM((keys, width), BF16),
            pltpu.VMEM((blocks, heads, rows, rows), F32),
            pltpu.VMEM((heads, rows, 128), F32),
            pltpu.VMEM((heads, rows, 128), F32),
            pltpu.VMEM((heads, rows, HEAD_DIM), F32),
        ],
        compiler_params=pltpu.CompilerParams(vmem_limit_bytes=60 << 20),
        cost_estimate=pl.CostEstimate(
            flops=4 * heads * rows * 1280 * 128,
            bytes_accessed=4 << 20,
            transcendentals=heads * rows * 1280,
        ),
        name="attention",
    )(doc_lengths, page_table, queries, *got)


def project_kernel(att_ref, mix_ref, wa_ref, wm_ref, send_ref, keep_ref):
    sent = send_ref.shape[0]
    total = nn(att_ref[...], wa_ref[...]) + nn(mix_ref[...], wm_ref[...])
    send_ref[...] = total[:sent].astype(BF16)
    keep_ref[...] = total[sent:]


def project(att, mix, wa, wm, start, width, tile):
    rows, depth = att.shape
    base = start // tile
    whole = pl.BlockSpec((rows, depth), lambda j: (0, 0))
    weight = pl.BlockSpec((depth, tile), lambda j: (0, base + j))
    out = pl.BlockSpec((rows // 2, tile), lambda j: (0, j))
    return pl.pallas_call(
        project_kernel,
        grid=(width // tile,),
        out_shape=(
            jax.ShapeDtypeStruct((rows // 2, width), BF16),
            jax.ShapeDtypeStruct((rows // 2, width), F32),
        ),
        in_specs=[whole, whole, weight, weight],
        out_specs=(out, out),
        compiler_params=pltpu.CompilerParams(vmem_limit_bytes=24 << 20),
        cost_estimate=pl.CostEstimate(
            flops=4 * rows * depth * width,
            bytes_accessed=4 * depth * width + 4 * rows * depth + 4 * rows * width,
            transcendentals=0,
        ),
        name="project",
    )(att, mix, wa, wm)


def shards(
    n_ctx,
    n_tp,
    queries,
    key_pages,
    value_pages,
    mixer_input,
    state_write,
    state_read,
    log_decay,
    skip_gain,
    doc_lengths,
    page_table,
    attention_weight,
    mixer_weight,
):
    tok_rows = queries.shape[0]
    page_len = key_pages.shape[1]
    chips = n_ctx // 2

    def between_chips(a, j):
        return lax.ppermute(a, "ctx", [(i, i ^ (2 * j)) for i in range(n_ctx)])

    def other_core(a):
        return lax.ppermute(a, "ctx", [(i, i ^ 1) for i in range(n_ctx)])

    width = key_pages.shape[2]
    kv = jnp.stack([key_pages.reshape(-1, width), value_pages.reshape(-1, width)])
    far = [kv] + [between_chips(kv, j) for j in range(1, chips)]

    base, st, eg = mixer_local(
        doc_lengths, skip_gain, mixer_input, state_write, state_read, log_decay
    )
    st_other = other_core(st)
    chip_state = compose(st, st_other)
    got_states = [between_chips(chip_state, j) for j in range(1, chips)]

    got = []
    for a in far:
        got += [a, other_core(a)]
    att = attention(page_len, doc_lengths, page_table, queries, got)

    entering = carry_in(got_states)
    mix = finish(base, state_read, eg, entering, other_core(entering), st_other)

    part = tok_rows // n_tp
    columns = attention_weight.shape[1]
    chunk = columns // 4
    pieces = []
    for start in range(0, columns, chunk):
        send, keep = project(att, mix, attention_weight, mixer_weight, start, chunk, 512)
        near = lax.ppermute(send, "tp", [(i, i ^ 1) for i in range(n_tp)])
        both = keep + near.astype(F32)
        last = lax.ppermute(both[part:].astype(BF16), "tp", [(i, i ^ 2) for i in range(n_tp)])
        pieces.append((both[:part] + last.astype(F32)).astype(BF16))
    return jnp.concatenate(pieces, axis=1)


def solution(mesh):
    placed = (
        P("ctx", "tp"),
        P("ctx", None, "tp"),
        P("ctx", None, "tp"),
        P("ctx", "tp"),
        P("ctx", "tp"),
        P("ctx", "tp"),
        P("tp", "ctx"),
        P("tp"),
        P(),
        P(),
        P("tp", None),
        P("tp", None),
    )
    return jax.shard_map(
        functools.partial(shards, mesh.shape["ctx"], mesh.shape["tp"]),
        mesh=mesh,
        in_specs=placed,
        out_specs=P(("ctx", "tp"), None),
        check_vma=False,
    )
```

```python
import functools

import jax
import jax.numpy as jnp
from jax import lax
from jax.experimental import pallas as pl
from jax.experimental.pallas import tpu as pltpu
from jax.sharding import PartitionSpec as P

HEAD_DIM = 128
SSM_HEAD_DIM = 128
STATE = 128
LOG2E = 1.4426950408889634
LOW = -1e30
SHARES = (2, 2, 2, 1, 1)
F32 = jnp.float32
BF16 = jnp.bfloat16

MIB = 1 << 20
VMEM_SPEC = pl.BlockSpec(memory_space=pltpu.VMEM)
ANY_SPEC = pl.BlockSpec(memory_space=pl.ANY)
HBM_SPEC = pl.BlockSpec(memory_space=pltpu.HBM)


def in_hbm(a):
    return pltpu.with_memory_space_constraint(a, pltpu.HBM)


class Far:
    def __init__(self, array, space=pltpu.VMEM, lanes=None):
        self.array, self.lanes = array, lanes
        shape = array.shape if lanes is None else (array.shape[0], lanes.stop - lanes.start)
        self.scratch = space(shape, array.dtype)


def one_step(kernel, name, out_shape, far, near, scratch=(), cost=(0, 0, 0), room=6 * MIB, specs=None):
    flops, moved, exps = cost

    def body(*refs):
        given, refs = refs[: len(far)], refs[len(far) :]
        rest, held, sem = refs[: -len(far) - 1], refs[-len(far) - 1 : -1], refs[-1]
        copies = []
        for i, (f, src, dst) in enumerate(zip(far, given, held)):
            src = src if f.lanes is None else src.at[:, f.lanes]
            copies.append(pltpu.make_async_copy(src, dst, sem.at[i]))
        for c in copies:
            c.start()
        for c in copies:
            c.wait()
        kernel(*held, *rest)

    return pl.pallas_call(
        body,
        out_shape=tuple(out_shape),
        in_specs=[HBM_SPEC] * len(far) + (specs or [VMEM_SPEC] * len(near)),
        out_specs=(VMEM_SPEC,) * len(out_shape),
        scratch_shapes=[
            *scratch,
            *(f.scratch for f in far),
            pltpu.SemaphoreType.DMA((len(far),)),
        ],
        compiler_params=pltpu.CompilerParams(vmem_limit_bytes=room),
        cost_estimate=pl.CostEstimate(flops=flops, bytes_accessed=moved, transcendentals=exps),
        name=name,
    )(*(in_hbm(f.array) for f in far), *near)


def doc_ends_of(len_ref):
    ends, total = [], 0
    for i in range(len_ref.shape[0]):
        total = total + len_ref[i]
        ends.append(total)
    return ends


def doc_start(pos, ends):
    start = jnp.zeros_like(pos)
    for end in ends:
        start = jnp.where(pos >= end, end, start)
    return start


def row_slot(part, z):
    d = part ^ z
    return jnp.where(d == 1, 0, jnp.where(d == 3, 1, jnp.where(d == 0, 2, 3)))


def nt(a, b):
    return lax.dot_general(a, b, (((1,), (1,)), ((), ())), preferred_element_type=F32)


def nn(a, b):
    return lax.dot_general(a, b, (((1,), (0,)), ((), ())), preferred_element_type=F32)


def mixer_kernel(len_ref, skip_ref, x_ref, w_ref, r_ref, ld_ref, base_ref, st_ref, eg_ref):
    me = lax.axis_index("ctx")
    heads, rows = ld_ref.shape
    groups = w_ref.shape[1] // STATE
    per_group = heads // groups
    half = heads // 2
    first = me * rows
    ends = doc_ends_of(len_ref)
    ds = ld_ref[...]
    lane = lax.broadcasted_iota(jnp.int32, ds.shape, 1)
    shift = 1
    while shift < rows:
        ds = ds + jnp.where(lane >= shift, pltpu.roll(ds, shift, 1), 0.0)
        shift *= 2
    col = ds.T
    t_pos = first + lax.broadcasted_iota(jnp.int32, (rows, 1), 0)
    t_start = doc_start(t_pos, ends)
    s_pos = first + lax.broadcasted_iota(jnp.int32, (1, rows), 1)
    last = first + rows - 1
    last_start = doc_start(jnp.full((1, 1), last, jnp.int32), ends)
    visible = (s_pos <= t_pos) & (s_pos >= t_start)
    bias = jnp.where(visible, 0.0, LOW)
    eg_ref[...] = jnp.where(t_start < first, jnp.exp(col), 0.0)
    total = ds[:, rows - 1 : rows]
    end_weight = jnp.where(s_pos >= last_start, jnp.exp(total - ds), 0.0)
    gain = jnp.where(last_start < first, jnp.exp(total), 0.0)
    gain = jnp.broadcast_to(gain, (heads, SSM_HEAD_DIM)).astype(BF16)
    pad = jnp.zeros((st_ref.shape[1] - half * STATE - half, SSM_HEAD_DIM), BF16)
    for c in range(2):
        st_ref[c, half * STATE :, :] = jnp.concatenate(
            [gain[c * half : (c + 1) * half].astype(F32), pad.astype(F32)], axis=0
        ).astype(BF16)
    for g in range(groups):
        cols = slice(g * STATE, (g + 1) * STATE)
        write, read = w_ref[:, cols], r_ref[:, cols]
        inner = nt(read, write)
        write_t = write.astype(F32).T
        for h in range(g * per_group, (g + 1) * per_group):
            hc = slice(h * SSM_HEAD_DIM, (h + 1) * SSM_HEAD_DIM)
            x = x_ref[:, hc]
            decay = jnp.exp((col[:, h : h + 1] - ds[h : h + 1, :]) + bias)
            mixing = (decay * inner).astype(BF16)
            base_ref[:, hc] = nn(mixing, x) + skip_ref[h] * x.astype(F32)
            end_write = (write_t * end_weight[h : h + 1, :]).astype(BF16)
            c, i = divmod(h, half)
            st_ref[c, i * STATE : (i + 1) * STATE, :] = nn(end_write, x).astype(BF16)


def mixer_local(doc_lengths, skip_gain, x, w, r, ld):
    heads, rows = ld.shape
    half = heads // 2
    return one_step(
        mixer_kernel,
        "mixer_local",
        (
            jax.ShapeDtypeStruct(x.shape, F32),
            jax.ShapeDtypeStruct((2, half * STATE + 16, SSM_HEAD_DIM), BF16),
            jax.ShapeDtypeStruct((rows, heads), F32),
        ),
        (Far(doc_lengths, pltpu.SMEM), Far(skip_gain, pltpu.SMEM), Far(x), Far(w), Far(r), Far(ld)),
        (),
    )


def compose_kernel(mine_ref, other_ref, out_ref):
    core = lax.axis_index("ctx") & 1
    state_rows = out_ref.shape[0] - 16
    half = state_rows // STATE
    a, b = mine_ref[core].astype(F32), other_ref[core].astype(F32)
    first = jnp.where(core == 0, a, b)
    second = jnp.where(core == 0, b, a)
    for i in range(half):
        rows = slice(i * STATE, (i + 1) * STATE)
        gain = second[state_rows + i : state_rows + i + 1]
        out_ref[rows, :] = (gain * first[rows] + second[rows]).astype(BF16)
    out_ref[state_rows:, :] = (first[state_rows:] * second[state_rows:]).astype(BF16)


def compose(mine, other):
    return pl.pallas_call(
        compose_kernel,
        out_shape=jax.ShapeDtypeStruct(mine.shape[1:], BF16),
        in_specs=[VMEM_SPEC] * 2,
        out_specs=VMEM_SPEC,
        compiler_params=pltpu.CompilerParams(vmem_limit_bytes=4 * MIB),
        cost_estimate=pl.CostEstimate(flops=0, bytes_accessed=0, transcendentals=0),
        name="compose",
    )(mine, other)


def finish_kernel(r_ref, base_ref, eg_ref, st_ref, *refs):
    *got, out_ref, held = refs
    me = lax.axis_index("ctx")
    core, chip = me & 1, me // 2
    z = lax.axis_index("tp")
    rows = base_ref.shape[0]
    part = rows // 4
    state_rows = st_ref.shape[1] - 16
    half = state_rows // STATE
    groups = r_ref.shape[1] // STATE
    heads = 2 * half
    per_group = heads // groups
    for j in range(1, held.shape[0]):
        held[chip ^ j, core] = got[2 * j - 2][...]
        held[chip ^ j, core ^ 1] = got[2 * j - 1][...]

    for h in range(heads):
        c, i = divmod(h, half)
        hs = slice(i * STATE, (i + 1) * STATE)
        gs = slice(state_rows + i, state_rows + i + 1)

        def one(k, carry):
            return held[k, c, gs, :].astype(F32) * carry + held[k, c, hs, :].astype(F32)

        entering = lax.fori_loop(0, chip, one, jnp.zeros((STATE, SSM_HEAD_DIM), F32))
        prev = st_ref[c, hs, :].astype(F32)
        gain = st_ref[c, gs, :].astype(F32)
        carry = jnp.where(core == 1, gain * entering + prev, entering).astype(BF16)
        hc = slice(h * SSM_HEAD_DIM, (h + 1) * SSM_HEAD_DIM)
        g = h // per_group
        inter = nn(r_ref[:, g * STATE : (g + 1) * STATE], carry)
        res = (base_ref[:, hc] + eg_ref[:, h : h + 1] * inter).astype(BF16)
        for q in range(4):
            at = pl.multiple_of(row_slot(q, z) * part, part)
            out_ref[pl.ds(at, part), hc] = res[q * part : (q + 1) * part]


def finish(base, r, eg, st_other, got):
    chips = len(got) // 2 + 1
    return one_step(
        finish_kernel,
        "finish",
        (jax.ShapeDtypeStruct(base.shape, BF16),),
        (Far(r),),
        (base, eg, st_other, *got),
        scratch=[pltpu.VMEM((chips, 2) + got[0].shape, BF16)],
        room=(4 + chips) * MIB,
    )[0]


def attention_kernel(page_len, kv_head, len_ref, table_ref, q_ref, *refs):
    *got, _, _, out_ref, inv, kv, sem, sc, mx, ls, acc = refs
    me = lax.axis_index("ctx")
    z = lax.axis_index("tp")
    rows = q_ref.shape[0]
    part = rows // 4
    heads = q_ref.shape[1] // HEAD_DIM
    lanes = slice(kv_head * HEAD_DIM, (kv_head + 1) * HEAD_DIM)
    first = me * rows
    ends = doc_ends_of(len_ref)
    start0 = 0
    for end in ends:
        start0 = jnp.where(first >= end, end, start0)
    low_block = start0 // rows
    pages_block = rows // page_len

    def invert(l, _):
        inv[table_ref[l]] = l
        return 0

    lax.fori_loop(0, table_ref.shape[0], invert, 0)
    low_page, high_page = low_block * pages_block, (me + 1) * pages_block

    def page_copy(ref, slot, page):
        here = pl.ds(slot * page_len, page_len)
        there = pl.ds(pl.multiple_of(page * page_len, page_len), page_len)
        return pltpu.make_async_copy(ref.at[:, here, lanes], kv.at[:, there, :], sem.at[page])

    for j, ref in enumerate(got):
        for slot in range(ref.shape[1] // page_len):
            page = inv[(me ^ j) * (ref.shape[1] // page_len) + slot]

            @pl.when((page >= low_page) & (page < high_page))
            def _():
                page_copy(ref, slot, page).start()

    t_pos = first + lax.broadcasted_iota(jnp.int32, (rows, 1), 0)
    t_start = doc_start(t_pos, ends)
    scale = LOG2E * HEAD_DIM ** (-0.5)

    def scores(block, own):
        for i in range(pages_block):
            page_copy(got[0], 0, block * pages_block + i).wait()
        at = pl.ds(pl.multiple_of(block * rows, rows), rows)
        u_pos = block * rows + lax.broadcasted_iota(jnp.int32, (1, rows), 1)
        shown = u_pos >= t_start
        if own:
            shown = shown & (u_pos <= t_pos)
        for h in range(heads):
            s = nt(
                q_ref[:, h * HEAD_DIM : (h + 1) * HEAD_DIM],
                kv[0, at, :],
            )
            s = jnp.where(shown, s * scale, LOW)
            sc[block - low_block, h] = s
            top = s[:, :128]
            for k in range(128, rows, 128):
                top = jnp.maximum(top, s[:, k : k + 128])
            mx[h] = top if own else jnp.maximum(mx[h], top)

    scores(me, True)

    def earlier(block, _):
        scores(block, False)
        return 0

    lax.fori_loop(low_block, me, earlier, 0)
    for h in range(heads):
        mx[h] = jnp.broadcast_to(jnp.max(mx[h], axis=1, keepdims=True), (rows, 128))
    ls[...] = jnp.zeros_like(ls)
    acc[...] = jnp.zeros_like(acc)

    def weigh(block, _):
        at = pl.ds(pl.multiple_of(block * rows, rows), rows)
        for h in range(heads):
            m = mx[h]
            total = ls[h]
            pieces = []
            for k in range(0, rows, 128):
                w = jnp.exp2(sc[block - low_block, h, :, k : k + 128] - m)
                total = total + w
                pieces.append(w.astype(BF16))
            ls[h] = total
            acc[h] += nn(
                jnp.concatenate(pieces, axis=1), kv[1, at, :]
            )
        return 0

    lax.fori_loop(low_block, me + 1, weigh, 0)
    for h in range(heads):
        res = (acc[h] / jnp.sum(ls[h], axis=1, keepdims=True)).astype(BF16)
        for q in range(4):
            at = pl.multiple_of(row_slot(q, z) * part, part)
            out_ref[pl.ds(at, part), h * HEAD_DIM : (h + 1) * HEAD_DIM] = res[
                q * part : (q + 1) * part
            ]


def attention(page_len, doc_lengths, page_table, queries, got, ready, kv_head, kv_heads):
    rows = queries.shape[0]
    width = queries.shape[1] // kv_heads
    heads = width // HEAD_DIM
    out = jax.ShapeDtypeStruct((rows, width), BF16)
    keys = len(got) * got[0].shape[1]
    blocks = min(keys // rows, keys // 2 // rows + 1)
    return one_step(
        functools.partial(attention_kernel, page_len, kv_head),
        "attention",
        (out,),
        (
            Far(doc_lengths, pltpu.SMEM),
            Far(page_table, pltpu.SMEM),
            Far(queries, lanes=slice(kv_head * width, (kv_head + 1) * width)),
        ),
        (*got, *ready),
        specs=[ANY_SPEC] * (len(got) + len(ready)),
        scratch=[
            pltpu.SMEM((page_table.shape[0],), jnp.int32),
            pltpu.VMEM((2, keys, HEAD_DIM), BF16),
            pltpu.SemaphoreType.DMA((page_table.shape[0],)),
            pltpu.VMEM((blocks, heads, rows, rows), F32),
            pltpu.VMEM((heads, rows, 128), F32),
            pltpu.VMEM((heads, rows, 128), F32),
            pltpu.VMEM((heads, rows, HEAD_DIM), F32),
        ],
        cost=(64 * heads * rows * 1280 * 128, 4 << 20, heads * rows * 1280),
        room=5 * MIB + 4 * heads * rows * rows * blocks + 4 * keys * HEAD_DIM,
    )[0]


def fetch_kernel(pieces, *refs):
    *given, sem = refs
    given = given[1:]
    count = len(given) // 2
    copies = []
    for k in range(count):
        depth = given[k].shape[0] // pieces
        for i in range(pieces):
            here = slice(i * depth, (i + 1) * depth)
            copies.append(
                pltpu.make_async_copy(
                    given[k].at[here], given[count + k].at[here], sem.at[k * pieces + i]
                )
            )
    for c in copies:
        c.start()
    for c in copies:
        c.wait()


def fetch(after, *weights):
    return pl.pallas_call(
        functools.partial(fetch_kernel, 4),
        out_shape=tuple(jax.ShapeDtypeStruct(w.shape, w.dtype) for w in weights),
        in_specs=[ANY_SPEC] + [HBM_SPEC] * len(weights),
        out_specs=(VMEM_SPEC,) * len(weights),
        scratch_shapes=[pltpu.SemaphoreType.DMA((4 * len(weights),))],
        compiler_params=pltpu.CompilerParams(vmem_limit_bytes=1 * MIB),
        cost_estimate=pl.CostEstimate(
            flops=0, bytes_accessed=2 * sum(w.size for w in weights), transcendentals=0
        ),
        name="fetch",
    )(after, *(in_hbm(w) for w in weights))


def project_kernel(start, tile, count, *refs):
    att, (mix_ref, wa_ref, wm_ref), out = refs[:count], refs[count : count + 3], refs[count + 3 :]
    for send_ref, keep_ref in zip(out[::2], out[1::2]):
        sent, width = send_ref.shape
        for j in range(0, width, tile):
            here, there = slice(j, j + tile), slice(start + j, start + j + tile)
            total = nn(mix_ref[...], wm_ref[:, there])
            row = 0
            for a in att:
                total += nn(a[...], wa_ref[row : row + a.shape[1], there])
                row += a.shape[1]
            send_ref[:, here] = total[:sent].astype(BF16)
            keep_ref[:, here] = total[sent:]
        start += width


def project(att, mix, wa, wm, start, widths, tile):
    rows, depth = mix.shape
    out_shape = []
    for width in widths:
        out_shape.append(jax.ShapeDtypeStruct((rows // 2, width), BF16))
        out_shape.append(jax.ShapeDtypeStruct((rows // 2, width), F32))
    out = pl.pallas_call(
        functools.partial(project_kernel, start, tile, len(att)),
        out_shape=tuple(out_shape),
        in_specs=[VMEM_SPEC] * (len(att) + 3),
        out_specs=(VMEM_SPEC,) * len(out_shape),
        compiler_params=pltpu.CompilerParams(vmem_limit_bytes=4 * MIB),
        cost_estimate=pl.CostEstimate(
            flops=4 * rows * depth * sum(widths),
            bytes_accessed=6 * rows * sum(widths),
            transcendentals=0,
        ),
        name="project",
    )(*att, mix, wa, wm)
    return list(zip(out[::2], out[1::2]))


def shards(
    n_ctx,
    n_tp,
    queries,
    key_pages,
    value_pages,
    mixer_input,
    state_write,
    state_read,
    log_decay,
    skip_gain,
    doc_lengths,
    page_table,
    attention_weight,
    mixer_weight,
):
    tok_rows = queries.shape[0]
    page_len = key_pages.shape[1]
    chips = n_ctx // 2

    def between_chips(a, j):
        return lax.ppermute(a, "ctx", [(i, i ^ (2 * j)) for i in range(n_ctx)])

    def other_core(a):
        return lax.ppermute(a, "ctx", [(i, i ^ 1) for i in range(n_ctx)])

    width = key_pages.shape[2]
    kv = jnp.stack([key_pages.reshape(-1, width), value_pages.reshape(-1, width)])
    kv, mixer_input = lax.optimization_barrier((kv, mixer_input))
    far = [kv] + [between_chips(kv, j) for j in range(1, chips)]

    base, st, eg = mixer_local(
        doc_lengths, skip_gain, mixer_input, state_write, state_read, log_decay
    )
    st_other = other_core(st)
    chip_state = compose(st, st_other)
    ready = fetch(st, attention_weight, mixer_weight)
    far_states = [between_chips(chip_state, j) for j in range(1, chips)]

    far[1:], ready = lax.optimization_barrier((far[1:], ready))
    got = []
    for a in far:
        got += [a, other_core(a)]
    kv_heads = width // HEAD_DIM
    att = [
        attention(page_len, doc_lengths, page_table, queries, got, ready, i, kv_heads)
        for i in range(kv_heads)
    ]
    *far_states, att[0] = lax.optimization_barrier((*far_states, att[0]))
    got_states = []
    for a in far_states:
        got_states += [a, other_core(a)]
    mix = finish(base, state_read, eg, st_other, got_states)

    part = tok_rows // n_tp
    columns = attention_weight.shape[1]
    widths = [share * columns // 8 for share in SHARES]
    sums = project(att, mix, *ready, 0, widths[:1], 256)
    sums += project(att, mix, *ready, widths[0], widths[1:], 256)
    kept = [
        (keep, lax.ppermute(send, "tp", [(i, i ^ 1) for i in range(n_tp)])) for send, keep in sums
    ]
    pieces = []
    order = None
    for keep, near in kept:
        if order is not None:
            near, order = lax.optimization_barrier((near, order))
        both = keep + near.astype(F32)
        order = both[part:].astype(BF16)
        last = lax.ppermute(order, "tp", [(i, i ^ 2) for i in range(n_tp)])
        pieces.append((both[:part] + last.astype(F32)).astype(BF16))
    return jnp.concatenate(pieces, axis=1)


def solution(mesh):
    placed = (
        P("ctx", "tp"),
        P("ctx", None, "tp"),
        P("ctx", None, "tp"),
        P("ctx", "tp"),
        P("ctx", "tp"),
        P("ctx", "tp"),
        P("tp", "ctx"),
        P("tp"),
        P(),
        P(),
        P("tp", None),
        P("tp", None),
    )
    return jax.shard_map(
        functools.partial(shards, mesh.shape["ctx"], mesh.shape["tp"]),
        mesh=mesh,
        in_specs=placed,
        out_specs=P(("ctx", "tp"), None),
        check_vma=False,
    )
```

```python
import functools

import jax
import jax.numpy as jnp
from jax import lax
from jax.experimental import pallas as pl
from jax.experimental.pallas import tpu as pltpu
from jax.sharding import PartitionSpec as P

HEAD_DIM = 128
SSM_HEAD_DIM = 128
STATE = 128
LOG2E = 1.4426950408889634
LOW = -1e30
SHARES = (2, 2, 2, 2)
F32 = jnp.float32
BF16 = jnp.bfloat16

MIB = 1 << 20
VMEM_SPEC = pl.BlockSpec(memory_space=pltpu.VMEM)
ANY_SPEC = pl.BlockSpec(memory_space=pl.ANY)
HBM_SPEC = pl.BlockSpec(memory_space=pltpu.HBM)


def in_hbm(a):
    return pltpu.with_memory_space_constraint(a, pltpu.HBM)


class Far:
    def __init__(self, array, space=pltpu.VMEM, lanes=None):
        self.array, self.lanes = array, lanes
        shape = array.shape if lanes is None else (array.shape[0], lanes.stop - lanes.start)
        self.scratch = space(shape, array.dtype)


def one_step(kernel, name, out_shape, far, near, scratch=(), cost=(0, 0, 0), room=6 * MIB, specs=None):
    flops, moved, exps = cost

    def body(*refs):
        given, refs = refs[: len(far)], refs[len(far) :]
        rest, held, sem = refs[: -len(far) - 1], refs[-len(far) - 1 : -1], refs[-1]
        copies = []
        for i, (f, src, dst) in enumerate(zip(far, given, held)):
            src = src if f.lanes is None else src.at[:, f.lanes]
            copies.append(pltpu.make_async_copy(src, dst, sem.at[i]))
        for c in copies:
            c.start()
        for c in copies:
            c.wait()
        kernel(*held, *rest)

    return pl.pallas_call(
        body,
        out_shape=tuple(out_shape),
        in_specs=[HBM_SPEC] * len(far) + (specs or [VMEM_SPEC] * len(near)),
        out_specs=(VMEM_SPEC,) * len(out_shape),
        scratch_shapes=[
            *scratch,
            *(f.scratch for f in far),
            pltpu.SemaphoreType.DMA((max(len(far), 1),)),
        ],
        compiler_params=pltpu.CompilerParams(vmem_limit_bytes=room),
        cost_estimate=pl.CostEstimate(flops=flops, bytes_accessed=moved, transcendentals=exps),
        name=name,
    )(*(in_hbm(f.array) for f in far), *near)


def doc_ends_of(len_ref):
    ends, total = [], 0
    for i in range(len_ref.shape[0]):
        total = total + len_ref[i]
        ends.append(total)
    return ends


def doc_start(pos, ends):
    start = jnp.zeros_like(pos)
    for end in ends:
        start = jnp.where(pos >= end, end, start)
    return start


def row_slot(part, z):
    return 3 - (part ^ z)


def nt(a, b):
    return lax.dot_general(a, b, (((1,), (1,)), ((), ())), preferred_element_type=F32)


def nn(a, b):
    return lax.dot_general(a, b, (((1,), (0,)), ((), ())), preferred_element_type=F32)


def mixer_kernel(len_ref, skip_ref, x_ref, w_ref, r_ref, ld_ref, base_ref, st_ref, eg_ref):
    me = lax.axis_index("ctx")
    heads, rows = ld_ref.shape
    groups = w_ref.shape[1] // STATE
    per_group = heads // groups
    half = heads // 2
    first = me * rows
    ends = doc_ends_of(len_ref)
    ds = ld_ref[...]
    lane = lax.broadcasted_iota(jnp.int32, ds.shape, 1)
    shift = 1
    while shift < rows:
        ds = ds + jnp.where(lane >= shift, pltpu.roll(ds, shift, 1), 0.0)
        shift *= 2
    col = ds.T
    t_pos = first + lax.broadcasted_iota(jnp.int32, (rows, 1), 0)
    t_start = doc_start(t_pos, ends)
    s_pos = first + lax.broadcasted_iota(jnp.int32, (1, rows), 1)
    last = first + rows - 1
    last_start = doc_start(jnp.full((1, 1), last, jnp.int32), ends)
    visible = (s_pos <= t_pos) & (s_pos >= t_start)
    bias = jnp.where(visible, 0.0, LOW)
    eg_ref[...] = jnp.where(t_start < first, jnp.exp(col), 0.0)
    total = ds[:, rows - 1 : rows]
    end_weight = jnp.where(s_pos >= last_start, jnp.exp(total - ds), 0.0)
    gain = jnp.where(last_start < first, jnp.exp(total), 0.0)
    gain = jnp.broadcast_to(gain, (heads, SSM_HEAD_DIM)).astype(BF16)
    pad = jnp.zeros((st_ref.shape[1] - half * STATE - half, SSM_HEAD_DIM), BF16)
    for c in range(2):
        st_ref[c, half * STATE :, :] = jnp.concatenate(
            [gain[c * half : (c + 1) * half].astype(F32), pad.astype(F32)], axis=0
        ).astype(BF16)
    for g in range(groups):
        cols = slice(g * STATE, (g + 1) * STATE)
        write, read = w_ref[:, cols], r_ref[:, cols]
        inner = nt(read, write)
        write_t = write.astype(F32).T
        for h in range(g * per_group, (g + 1) * per_group):
            hc = slice(h * SSM_HEAD_DIM, (h + 1) * SSM_HEAD_DIM)
            x = x_ref[:, hc]
            decay = jnp.exp((col[:, h : h + 1] - ds[h : h + 1, :]) + bias)
            mixing = (decay * inner).astype(BF16)
            base_ref[:, hc] = nn(mixing, x) + skip_ref[h] * x.astype(F32)
            end_write = (write_t * end_weight[h : h + 1, :]).astype(BF16)
            c, i = divmod(h, half)
            st_ref[c, i * STATE : (i + 1) * STATE, :] = nn(end_write, x).astype(BF16)


def mixer_local(doc_lengths, skip_gain, x, w, r, ld):
    heads, rows = ld.shape
    half = heads // 2
    return one_step(
        mixer_kernel,
        "mixer_local",
        (
            jax.ShapeDtypeStruct(x.shape, F32),
            jax.ShapeDtypeStruct((2, half * STATE + 16, SSM_HEAD_DIM), BF16),
            jax.ShapeDtypeStruct((rows, heads), F32),
        ),
        (Far(doc_lengths, pltpu.SMEM), Far(skip_gain, pltpu.SMEM), Far(x), Far(w), Far(r), Far(ld)),
        (),
    )


def compose_kernel(mine_ref, other_ref, out_ref):
    core = lax.axis_index("ctx") & 1
    state_rows = out_ref.shape[0] - 16
    half = state_rows // STATE
    a, b = mine_ref[core].astype(F32), other_ref[core].astype(F32)
    first = jnp.where(core == 0, a, b)
    second = jnp.where(core == 0, b, a)
    for i in range(half):
        rows = slice(i * STATE, (i + 1) * STATE)
        gain = second[state_rows + i : state_rows + i + 1]
        out_ref[rows, :] = (gain * first[rows] + second[rows]).astype(BF16)
    out_ref[state_rows:, :] = (first[state_rows:] * second[state_rows:]).astype(BF16)


def compose(mine, other):
    return pl.pallas_call(
        compose_kernel,
        out_shape=jax.ShapeDtypeStruct(mine.shape[1:], BF16),
        in_specs=[VMEM_SPEC] * 2,
        out_specs=VMEM_SPEC,
        compiler_params=pltpu.CompilerParams(vmem_limit_bytes=4 * MIB),
        cost_estimate=pl.CostEstimate(flops=0, bytes_accessed=0, transcendentals=0),
        name="compose",
    )(mine, other)


def finish_kernel(r_ref, base_ref, eg_ref, st_ref, *refs):
    *got, out_ref, held, carry = refs
    me = lax.axis_index("ctx")
    core, chip = me & 1, me // 2
    z = lax.axis_index("tp")
    rows = base_ref.shape[0]
    part = rows // 4
    state_rows = st_ref.shape[1] - 16
    half = state_rows // STATE
    groups = r_ref.shape[1] // STATE
    heads = 2 * half
    per_group = heads // groups
    for j in range(1, held.shape[0]):
        held[chip ^ j, core] = got[2 * j - 2][...]
        held[chip ^ j, core ^ 1] = got[2 * j - 1][...]
    carry[...] = jnp.zeros_like(carry)

    def where(h):
        c, i = divmod(h, half)
        return c, slice(i * STATE, (i + 1) * STATE), slice(state_rows + i, state_rows + i + 1)

    def one(k, _):
        for h in range(heads):
            c, hs, gs = where(h)
            carry[h] = held[k, c, gs, :].astype(F32) * carry[h] + held[k, c, hs, :].astype(F32)
        return 0

    lax.fori_loop(0, chip, one, 0)

    @pl.when(core == 1)
    def _():
        for h in range(heads):
            c, hs, gs = where(h)
            carry[h] = st_ref[c, gs, :].astype(F32) * carry[h] + st_ref[c, hs, :].astype(F32)

    for h in range(heads):
        hc = slice(h * SSM_HEAD_DIM, (h + 1) * SSM_HEAD_DIM)
        g = h // per_group
        inter = nn(r_ref[:, g * STATE : (g + 1) * STATE], carry[h].astype(BF16))
        res = (base_ref[:, hc] + eg_ref[:, h : h + 1] * inter).astype(BF16)
        for q in range(4):
            at = pl.multiple_of(row_slot(q, z) * part, part)
            out_ref[pl.ds(at, part), hc] = res[q * part : (q + 1) * part]


def finish(base, r, eg, st_other, got):
    chips = len(got) // 2 + 1
    heads = base.shape[1] // SSM_HEAD_DIM
    return one_step(
        finish_kernel,
        "finish",
        (jax.ShapeDtypeStruct(base.shape, BF16),),
        (),
        (r, base, eg, st_other, *got),
        scratch=[
            pltpu.VMEM((chips, 2) + got[0].shape, BF16),
            pltpu.VMEM((heads, STATE, SSM_HEAD_DIM), F32),
        ],
        room=(4 + chips) * MIB,
    )[0]


def attention_kernel(page_len, together, len_ref, table_ref, q_ref, *refs):
    *got, weight_ref, out_ref, ready_ref, inv, kv, sc, mx, ls, acc, weight_sem = refs
    pieces = weight_sem.shape[0]
    depth = weight_ref.shape[0] // pieces
    fetches = []
    for i in range(pieces):
        here = slice(i * depth, (i + 1) * depth)
        fetches.append(
            pltpu.make_async_copy(weight_ref.at[here], ready_ref.at[here], weight_sem.at[i])
        )
    for f in fetches:
        f.start()
    me = lax.axis_index("ctx")
    z = lax.axis_index("tp")
    rows = q_ref.shape[0]
    part = rows // 4
    heads = q_ref.shape[1] // HEAD_DIM
    group = heads // (kv.shape[2] // HEAD_DIM)
    first = me * rows
    ends = doc_ends_of(len_ref)
    start0 = 0
    for end in ends:
        start0 = jnp.where(first >= end, end, start0)
    low_block = start0 // rows

    def invert(l, _):
        inv[table_ref[l]] = l
        return 0

    lax.fori_loop(0, table_ref.shape[0], invert, 0, unroll=8)
    for j, ref in enumerate(got):
        pages = ref.shape[1] // page_len
        for slot in range(pages):
            page = inv[(me ^ j) * pages + slot]
            there = pl.ds(pl.multiple_of(page * page_len, page_len), page_len)
            here = slice(slot * page_len, (slot + 1) * page_len)
            for i in range(2):
                kv[i, there, :] = ref[i, here, :]

    t_pos = first + lax.broadcasted_iota(jnp.int32, (rows, 1), 0)
    t_start = doc_start(t_pos, ends)
    scale = LOG2E * HEAD_DIM ** (-0.5)

    def lanes(h):
        return slice(h // group * HEAD_DIM, (h // group + 1) * HEAD_DIM)

    for h0 in range(0, heads, together):
        some = range(h0, h0 + together)

        def scores(block, own):
            at = pl.ds(pl.multiple_of(block * rows, rows), rows)
            u_pos = block * rows + lax.broadcasted_iota(jnp.int32, (1, rows), 1)
            shown = u_pos >= t_start
            if own:
                shown = shown & (u_pos <= t_pos)
            for h in some:
                s = nt(q_ref[:, h * HEAD_DIM : (h + 1) * HEAD_DIM], kv[0, at, lanes(h)])
                s = jnp.where(shown, s * scale, LOW)
                sc[block - low_block, h - h0] = s
                top = s[:, :128]
                for k in range(128, rows, 128):
                    top = jnp.maximum(top, s[:, k : k + 128])
                mx[h - h0] = top if own else jnp.maximum(mx[h - h0], top)

        scores(me, True)

        def earlier(block, _):
            scores(block, False)
            return 0

        lax.fori_loop(low_block, me, earlier, 0)
        for i in range(together):
            mx[i] = jnp.broadcast_to(jnp.max(mx[i], axis=1, keepdims=True), (rows, 128))

        def weigh(block, own):
            at = pl.ds(pl.multiple_of(block * rows, rows), rows)
            for h in some:
                i = h - h0
                m = mx[i]
                total, pieces = None, []
                for k in range(0, rows, 128):
                    w = jnp.exp2(sc[block - low_block, i, :, k : k + 128] - m)
                    total = w if total is None else total + w
                    pieces.append(w.astype(BF16))
                term = nn(jnp.concatenate(pieces, axis=1), kv[1, at, lanes(h)])
                ls[i] = total if own else ls[i] + total
                acc[i] = term if own else acc[i] + term

        weigh(me, True)

        def weigh_earlier(block, _):
            weigh(block, False)
            return 0

        lax.fori_loop(low_block, me, weigh_earlier, 0)
        for h in some:
            inverse = 1.0 / jnp.sum(ls[h - h0], axis=1, keepdims=True)
            res = (acc[h - h0] * inverse).astype(BF16)
            for q in range(4):
                at = pl.multiple_of(row_slot(q, z) * part, part)
                out_ref[pl.ds(at, part), h * HEAD_DIM : (h + 1) * HEAD_DIM] = res[
                    q * part : (q + 1) * part
                ]
    for f in fetches:
        f.wait()


def attention(page_len, doc_lengths, page_table, queries, got, weight):
    rows = queries.shape[0]
    heads = queries.shape[1] // HEAD_DIM
    keys = len(got) * got[0].shape[1]
    width = got[0].shape[2]
    blocks = min(keys // rows, keys // 2 // rows + 1)
    block_bytes = 4 * rows * rows * blocks
    together = heads
    while together > 1 and together * block_bytes > 12 * MIB:
        together //= 2
    return one_step(
        functools.partial(attention_kernel, page_len, together),
        "attention",
        (
            jax.ShapeDtypeStruct(queries.shape, BF16),
            jax.ShapeDtypeStruct(weight.shape, weight.dtype),
        ),
        (Far(doc_lengths, pltpu.SMEM), Far(page_table, pltpu.SMEM)),
        (queries, *got, in_hbm(weight)),
        specs=[VMEM_SPEC] * (1 + len(got)) + [HBM_SPEC],
        scratch=[
            pltpu.SMEM((page_table.shape[0],), jnp.int32),
            pltpu.VMEM((2, keys, width), BF16),
            pltpu.VMEM((blocks, together, rows, rows), F32),
            pltpu.VMEM((together, rows, 128), F32),
            pltpu.VMEM((together, rows, 128), F32),
            pltpu.VMEM((together, rows, HEAD_DIM), F32),
            pltpu.SemaphoreType.DMA((4,)),
        ],
        cost=(128 * heads * rows * 1280 * 128, 4 << 20, heads * rows * 1280),
        room=6 * MIB + together * block_bytes + 4 * keys * width,
    )


def fetch_kernel(pieces, *refs):
    *given, sem = refs
    given = given[1:]
    count = len(given) // 2
    copies = []
    for k in range(count):
        depth = given[k].shape[0] // pieces
        for i in range(pieces):
            here = slice(i * depth, (i + 1) * depth)
            copies.append(
                pltpu.make_async_copy(
                    given[k].at[here], given[count + k].at[here], sem.at[k * pieces + i]
                )
            )
    for c in copies:
        c.start()
    for c in copies:
        c.wait()


def fetch(after, *weights):
    return pl.pallas_call(
        functools.partial(fetch_kernel, 4),
        out_shape=tuple(jax.ShapeDtypeStruct(w.shape, w.dtype) for w in weights),
        in_specs=[ANY_SPEC] + [HBM_SPEC] * len(weights),
        out_specs=(VMEM_SPEC,) * len(weights),
        scratch_shapes=[pltpu.SemaphoreType.DMA((4 * len(weights),))],
        compiler_params=pltpu.CompilerParams(vmem_limit_bytes=1 * MIB),
        cost_estimate=pl.CostEstimate(
            flops=0, bytes_accessed=2 * sum(w.size for w in weights), transcendentals=0
        ),
        name="fetch",
    )(after, *(in_hbm(w) for w in weights))


def project_kernel(start, tile, joined, att_ref, mix_ref, wa_ref, wm_ref, *out):
    *other, send_ref, keep_ref = out
    part = keep_ref.shape[0]
    at = 0
    for keep_other in other[-1:] if joined else other[1::2]:
        for j in range(0, keep_other.shape[1], tile):
            here, there = slice(j, j + tile), slice(start + at, start + at + tile)
            own = slice(at, at + tile)
            total = nn(att_ref[...], wa_ref[:, there]) + nn(mix_ref[...], wm_ref[:, there])
            through = total[:part].astype(BF16)
            if joined:
                send_ref[:part, own] = through
                send_ref[part:, own] = total[2 * part : 3 * part].astype(BF16)
            else:
                other[2 * [o is keep_other for o in other[1::2]].index(True)][:, here] = through
                send_ref[:, own] = total[2 * part : 3 * part].astype(BF16)
            keep_other[:, here] = total[part : 2 * part]
            keep_ref[:, own] = total[3 * part :]
            at += tile


def project(att, mix, wa, wm, start, widths, tile, joined):
    rows, depth = mix.shape
    part, width = rows // 4, sum(widths)
    out_shape = []
    for w in widths:
        if not joined:
            out_shape.append(jax.ShapeDtypeStruct((part, w), BF16))
        out_shape.append(jax.ShapeDtypeStruct((part, w), F32))
    out_shape.append(jax.ShapeDtypeStruct((2 * part if joined else part, width), BF16))
    out_shape.append(jax.ShapeDtypeStruct((part, width), F32))
    return pl.pallas_call(
        functools.partial(project_kernel, start, tile, joined),
        out_shape=tuple(out_shape),
        in_specs=[VMEM_SPEC] * 4,
        out_specs=(VMEM_SPEC,) * len(out_shape),
        compiler_params=pltpu.CompilerParams(vmem_limit_bytes=4 * MIB),
        cost_estimate=pl.CostEstimate(
            flops=4 * rows * depth * width, bytes_accessed=6 * rows * width, transcendentals=0
        ),
        name="project",
    )(att, mix, wa, wm)


def shards(
    n_ctx,
    n_tp,
    queries,
    key_pages,
    value_pages,
    mixer_input,
    state_write,
    state_read,
    log_decay,
    skip_gain,
    doc_lengths,
    page_table,
    attention_weight,
    mixer_weight,
):
    tok_rows = queries.shape[0]
    page_len = key_pages.shape[1]
    chips = n_ctx // 2

    def between_chips(a, j):
        return lax.ppermute(a, "ctx", [(i, i ^ (2 * j)) for i in range(n_ctx)])

    def other_core(a):
        return lax.ppermute(a, "ctx", [(i, i ^ 1) for i in range(n_ctx)])

    width = key_pages.shape[2]
    kv = jnp.stack([key_pages.reshape(-1, width), value_pages.reshape(-1, width)])
    kv, mixer_input = lax.optimization_barrier((kv, mixer_input))
    far = [kv] + [between_chips(kv, j) for j in range(1, chips)]

    base, st, eg = mixer_local(
        doc_lengths, skip_gain, mixer_input, state_write, state_read, log_decay
    )
    st_other = other_core(st)
    chip_state = compose(st, st_other)
    near_weight, near_queries, near_read = fetch(
        st, attention_weight, queries, state_read
    )
    far_states = [between_chips(chip_state, j) for j in range(1, chips)]

    far[1:], near_queries = lax.optimization_barrier((far[1:], near_queries))
    got = []
    for a in far:
        got += [a, other_core(a)]
    att, far_weight = attention(
        page_len, doc_lengths, page_table, near_queries, got, mixer_weight
    )
    *far_states, att = lax.optimization_barrier((*far_states, att))
    got_states = []
    for a in far_states:
        got_states += [a, other_core(a)]
    mix = finish(base, near_read, eg, st_other, got_states)

    part = tok_rows // n_tp
    columns = attention_weight.shape[1]
    widths = [share * columns // 8 for share in SHARES]
    weights = (near_weight, far_weight)

    def neighbour(a):
        return lax.ppermute(a, "tp", [(i, i ^ 1) for i in range(n_tp)])

    def across(a):
        return lax.ppermute(a, "tp", [(i, i ^ 2) for i in range(n_tp)])

    keep_other, send, keep = project(att, mix, *weights, 0, widths[:1], 256, True)
    send, mix = lax.optimization_barrier((send, mix))
    *other, send_rest, keep_rest = project(
        att, mix, *weights, widths[0], widths[1:], 256, False
    )
    near = neighbour(send)
    near_other = [near[:part]] + [neighbour(a) for a in other[::2]]
    keep_other = [keep_other] + other[1::2]
    last, order = [], None
    for k in range(len(widths)):
        if order is not None:
            near_other[k], order = lax.optimization_barrier((near_other[k], order))
        both = keep_other[k] + near_other[k].astype(F32)

        order = both.astype(BF16)
        last.append(across(order))
        if k == 99:
            send_rest, order = lax.optimization_barrier((send_rest, order))
    near_rest = neighbour(send_rest)
    parts = [(keep, near[part:], last[0])]
    at = 0
    for a, width in zip(last[1:], widths[1:]):
        parts.append((keep_rest[:, at : at + width], near_rest[:, at : at + width], a))
        at += width
    pieces, done = [], None
    for a, b, c in parts:

        done = (a + b.astype(F32) + c.astype(F32)).astype(BF16)
        pieces.append(done)
    return jnp.concatenate(pieces, axis=1)


def solution(mesh):
    placed = (
        P("ctx", "tp"),
        P("ctx", None, "tp"),
        P("ctx", None, "tp"),
        P("ctx", "tp"),
        P("ctx", "tp"),
        P("ctx", "tp"),
        P("tp", "ctx"),
        P("tp"),
        P(),
        P(),
        P("tp", None),
        P("tp", None),
    )
    return jax.shard_map(
        functools.partial(shards, mesh.shape["ctx"], mesh.shape["tp"]),
        mesh=mesh,
        in_specs=placed,
        out_specs=P(("ctx", "tp"), None),
        check_vma=False,
    )
```

```python
import functools

import jax
import jax.numpy as jnp
from jax import lax
from jax.experimental import pallas as pl
from jax.experimental.pallas import tpu as pltpu
from jax.sharding import PartitionSpec as P

HEAD_DIM = 128
SSM_HEAD_DIM = 128
STATE = 128
LOG2E = 1.4426950408889634
LOW = -1e30
SHARES = (2, 2, 4)
F32 = jnp.float32
BF16 = jnp.bfloat16

MIB = 1 << 20
VMEM_SPEC = pl.BlockSpec(memory_space=pltpu.VMEM)
ANY_SPEC = pl.BlockSpec(memory_space=pl.ANY)
HBM_SPEC = pl.BlockSpec(memory_space=pltpu.HBM)


def in_hbm(a):
    return pltpu.with_memory_space_constraint(a, pltpu.HBM)


class Far:
    def __init__(self, array, space=pltpu.VMEM, lanes=None):
        self.array, self.lanes = array, lanes
        shape = array.shape if lanes is None else (array.shape[0], lanes.stop - lanes.start)
        self.scratch = space(shape, array.dtype)


def one_step(kernel, name, out_shape, far, near, scratch=(), cost=(0, 0, 0), room=6 * MIB, specs=None):
    flops, moved, exps = cost

    def body(*refs):
        given, refs = refs[: len(far)], refs[len(far) :]
        rest, held, sem = refs[: -len(far) - 1], refs[-len(far) - 1 : -1], refs[-1]
        copies = []
        for i, (f, src, dst) in enumerate(zip(far, given, held)):
            src = src if f.lanes is None else src.at[:, f.lanes]
            copies.append(pltpu.make_async_copy(src, dst, sem.at[i]))
        for c in copies:
            c.start()
        for c in copies:
            c.wait()
        kernel(*held, *rest)

    return pl.pallas_call(
        body,
        out_shape=tuple(out_shape),
        in_specs=[HBM_SPEC] * len(far) + (specs or [VMEM_SPEC] * len(near)),
        out_specs=(VMEM_SPEC,) * len(out_shape),
        scratch_shapes=[
            *scratch,
            *(f.scratch for f in far),
            pltpu.SemaphoreType.DMA((max(len(far), 1),)),
        ],
        compiler_params=pltpu.CompilerParams(vmem_limit_bytes=room),
        cost_estimate=pl.CostEstimate(flops=flops, bytes_accessed=moved, transcendentals=exps),
        name=name,
    )(*(in_hbm(f.array) for f in far), *near)


def doc_ends_of(len_ref):
    ends, total = [], 0
    for i in range(len_ref.shape[0]):
        total = total + len_ref[i]
        ends.append(total)
    return ends


def doc_start(pos, ends):
    start = jnp.zeros_like(pos)
    for end in ends:
        start = jnp.where(pos >= end, end, start)
    return start


def row_slot(part, z):
    return 3 - (part ^ z)


def nt(a, b):
    return lax.dot_general(a, b, (((1,), (1,)), ((), ())), preferred_element_type=F32)


def nn(a, b):
    return lax.dot_general(a, b, (((1,), (0,)), ((), ())), preferred_element_type=F32)


def mixer_kernel(len_ref, skip_ref, x_ref, w_ref, r_ref, ld_ref, base_ref, st_ref, eg_ref):
    me = lax.axis_index("ctx")
    heads, rows = ld_ref.shape
    groups = w_ref.shape[1] // STATE
    per_group = heads // groups
    half = heads // 2
    first = me * rows
    ends = doc_ends_of(len_ref)
    ds = ld_ref[...]
    lane = lax.broadcasted_iota(jnp.int32, ds.shape, 1)
    shift = 1
    while shift < rows:
        ds = ds + jnp.where(lane >= shift, pltpu.roll(ds, shift, 1), 0.0)
        shift *= 2
    col = ds.T
    t_pos = first + lax.broadcasted_iota(jnp.int32, (rows, 1), 0)
    t_start = doc_start(t_pos, ends)
    s_pos = first + lax.broadcasted_iota(jnp.int32, (1, rows), 1)
    last = first + rows - 1
    last_start = doc_start(jnp.full((1, 1), last, jnp.int32), ends)
    visible = (s_pos <= t_pos) & (s_pos >= t_start)
    bias = jnp.where(visible, 0.0, LOW)
    eg_ref[...] = jnp.where(t_start < first, jnp.exp(col), 0.0)
    total = ds[:, rows - 1 : rows]
    end_weight = jnp.where(s_pos >= last_start, jnp.exp(total - ds), 0.0)
    gain = jnp.where(last_start < first, jnp.exp(total), 0.0)
    gain = jnp.broadcast_to(gain, (heads, SSM_HEAD_DIM)).astype(BF16)
    pad = jnp.zeros((st_ref.shape[1] - half * STATE - half, SSM_HEAD_DIM), BF16)
    for c in range(2):
        st_ref[c, half * STATE :, :] = jnp.concatenate(
            [gain[c * half : (c + 1) * half].astype(F32), pad.astype(F32)], axis=0
        ).astype(BF16)
    for g in range(groups):
        cols = slice(g * STATE, (g + 1) * STATE)
        write, read = w_ref[:, cols], r_ref[:, cols]
        inner = nt(read, write)
        write_t = write.astype(F32).T
        for h in range(g * per_group, (g + 1) * per_group):
            hc = slice(h * SSM_HEAD_DIM, (h + 1) * SSM_HEAD_DIM)
            x = x_ref[:, hc]
            decay = jnp.exp((col[:, h : h + 1] - ds[h : h + 1, :]) + bias)
            mixing = (decay * inner).astype(BF16)
            base_ref[:, hc] = nn(mixing, x) + skip_ref[h] * x.astype(F32)
            end_write = (write_t * end_weight[h : h + 1, :]).astype(BF16)
            c, i = divmod(h, half)
            st_ref[c, i * STATE : (i + 1) * STATE, :] = nn(end_write, x).astype(BF16)


def mixer_local(doc_lengths, skip_gain, x, w, r, ld):
    heads, rows = ld.shape
    half = heads // 2
    return one_step(
        mixer_kernel,
        "mixer_local",
        (
            jax.ShapeDtypeStruct(x.shape, F32),
            jax.ShapeDtypeStruct((2, half * STATE + 16, SSM_HEAD_DIM), BF16),
            jax.ShapeDtypeStruct((rows, heads), F32),
        ),
        (Far(doc_lengths, pltpu.SMEM), Far(skip_gain, pltpu.SMEM), Far(x), Far(w), Far(r), Far(ld)),
        (),
    )


def compose_kernel(mine_ref, other_ref, out_ref):
    core = lax.axis_index("ctx") & 1
    state_rows = out_ref.shape[0] - 16
    half = state_rows // STATE
    a, b = mine_ref[core].astype(F32), other_ref[core].astype(F32)
    first = jnp.where(core == 0, a, b)
    second = jnp.where(core == 0, b, a)
    for i in range(half):
        rows = slice(i * STATE, (i + 1) * STATE)
        gain = second[state_rows + i : state_rows + i + 1]
        out_ref[rows, :] = (gain * first[rows] + second[rows]).astype(BF16)
    out_ref[state_rows:, :] = (first[state_rows:] * second[state_rows:]).astype(BF16)


def compose(mine, other):
    return pl.pallas_call(
        compose_kernel,
        out_shape=jax.ShapeDtypeStruct(mine.shape[1:], BF16),
        in_specs=[VMEM_SPEC] * 2,
        out_specs=VMEM_SPEC,
        compiler_params=pltpu.CompilerParams(vmem_limit_bytes=4 * MIB),
        cost_estimate=pl.CostEstimate(flops=0, bytes_accessed=0, transcendentals=0),
        name="compose",
    )(mine, other)


def finish_kernel(r_ref, base_ref, eg_ref, st_ref, *refs):
    *got, out_ref, held, carry = refs
    me = lax.axis_index("ctx")
    core, chip = me & 1, me // 2
    z = lax.axis_index("tp")
    rows = base_ref.shape[0]
    part = rows // 4
    state_rows = st_ref.shape[1] - 16
    half = state_rows // STATE
    groups = r_ref.shape[1] // STATE
    heads = 2 * half
    per_group = heads // groups
    for j in range(1, held.shape[0]):
        held[chip ^ j, core] = got[2 * j - 2][...]
        held[chip ^ j, core ^ 1] = got[2 * j - 1][...]
    carry[...] = jnp.zeros_like(carry)

    def where(h):
        c, i = divmod(h, half)
        return c, slice(i * STATE, (i + 1) * STATE), slice(state_rows + i, state_rows + i + 1)

    def one(k, _):
        for h in range(heads):
            c, hs, gs = where(h)
            carry[h] = held[k, c, gs, :].astype(F32) * carry[h] + held[k, c, hs, :].astype(F32)
        return 0

    lax.fori_loop(0, chip, one, 0)

    @pl.when(core == 1)
    def _():
        for h in range(heads):
            c, hs, gs = where(h)
            carry[h] = st_ref[c, gs, :].astype(F32) * carry[h] + st_ref[c, hs, :].astype(F32)

    for h in range(heads):
        hc = slice(h * SSM_HEAD_DIM, (h + 1) * SSM_HEAD_DIM)
        g = h // per_group
        inter = nn(r_ref[:, g * STATE : (g + 1) * STATE], carry[h].astype(BF16))
        res = (base_ref[:, hc] + eg_ref[:, h : h + 1] * inter).astype(BF16)
        for q in range(4):
            at = pl.multiple_of(row_slot(q, z) * part, part)
            out_ref[pl.ds(at, part), hc] = res[q * part : (q + 1) * part]


def finish(base, r, eg, st_other, got):
    chips = len(got) // 2 + 1
    heads = base.shape[1] // SSM_HEAD_DIM
    return one_step(
        finish_kernel,
        "finish",
        (jax.ShapeDtypeStruct(base.shape, BF16),),
        (),
        (r, base, eg, st_other, *got),
        scratch=[
            pltpu.VMEM((chips, 2) + got[0].shape, BF16),
            pltpu.VMEM((heads, STATE, SSM_HEAD_DIM), F32),
        ],
        room=(4 + chips) * MIB,
    )[0]


def attention_kernel(page_len, later, len_ref, table_ref, q_ref, *refs):
    if later:
        kv, out_ref, qs, sc, mx, ls, acc = refs
    else:
        *got, weight_ref, out_ref, kv, ready_ref, inv, qs, sc, mx, ls, acc, weight_sem = refs
        pieces = weight_sem.shape[0]
        depth = weight_ref.shape[0] // pieces
        fetches = []
        for i in range(pieces):
            here = slice(i * depth, (i + 1) * depth)
            fetches.append(
                pltpu.make_async_copy(weight_ref.at[here], ready_ref.at[here], weight_sem.at[i])
            )
        for f in fetches:
            f.start()
    me = lax.axis_index("ctx")
    z = lax.axis_index("tp")
    keys = q_ref.shape[0]
    rows = keys // 2
    part = rows // 2
    kv_heads = kv.shape[2] // HEAD_DIM
    group = q_ref.shape[1] // HEAD_DIM // kv_heads
    stacked = group * rows
    ends = doc_ends_of(len_ref)
    start0 = 0
    for end in ends:
        start0 = jnp.where(me * keys >= end, end, start0)
    low_block = start0 // keys
    side = z // 2 if later else 1 - z // 2

    if not later:

        def invert(l, _):
            inv[table_ref[l]] = l
            return 0

        lax.fori_loop(0, table_ref.shape[0], invert, 0, unroll=8)
        for j, ref in enumerate(got):
            pages = ref.shape[1] // page_len
            for slot in range(pages):
                page = inv[(me ^ j) * pages + slot]
                there = pl.ds(pl.multiple_of(page * page_len, page_len), page_len)
                here = slice(slot * page_len, (slot + 1) * page_len)
                for i in range(2):
                    kv[i, there, :] = ref[i, here, :]

    here = pl.ds(pl.multiple_of(side * rows, rows), rows)
    for h in range(kv_heads * group):
        g, i = divmod(h, group)
        qs[g, i * rows : (i + 1) * rows, :] = q_ref[here, h * HEAD_DIM : (h + 1) * HEAD_DIM]
    row = lax.rem(lax.broadcasted_iota(jnp.int32, (stacked, 1), 0), rows)
    t_pos = me * keys + side * rows + row
    t_start = doc_start(t_pos, ends)
    scale = LOG2E * HEAD_DIM ** (-0.5)

    def lanes(g):
        return slice(g * HEAD_DIM, (g + 1) * HEAD_DIM)

    def scores(block, own):
        at = pl.ds(pl.multiple_of(block * keys, keys), keys)
        u_pos = block * keys + lax.broadcasted_iota(jnp.int32, (1, keys), 1)
        shown = u_pos >= t_start
        if own:
            shown = shown & (u_pos <= t_pos)
        for g in range(kv_heads):
            s = nt(qs[g], kv[0, at, lanes(g)])
            s = jnp.where(shown, s * scale, LOW)
            sc[block - low_block, g] = s
            top = s[:, :128]
            for k in range(128, keys, 128):
                top = jnp.maximum(top, s[:, k : k + 128])
            mx[g] = top if own else jnp.maximum(mx[g], top)

    scores(me, True)

    def earlier(block, _):
        scores(block, False)
        return 0

    lax.fori_loop(low_block, me, earlier, 0)
    for g in range(kv_heads):
        mx[g] = jnp.broadcast_to(jnp.max(mx[g], axis=1, keepdims=True), (stacked, 128))

    def weigh(block, own):
        at = pl.ds(pl.multiple_of(block * keys, keys), keys)
        for g in range(kv_heads):
            m = mx[g]
            total, pieces = None, []
            for k in range(0, keys, 128):
                w = jnp.exp2(sc[block - low_block, g, :, k : k + 128] - m)
                total = w if total is None else total + w
                pieces.append(w.astype(BF16))
            term = nn(jnp.concatenate(pieces, axis=1), kv[1, at, lanes(g)])
            ls[g] = total if own else ls[g] + total
            acc[g] = term if own else acc[g] + term

    weigh(me, True)

    def weigh_earlier(block, _):
        weigh(block, False)
        return 0

    lax.fori_loop(low_block, me, weigh_earlier, 0)
    for g in range(kv_heads):
        inverse = 1.0 / jnp.sum(ls[g], axis=1, keepdims=True)
        res = (acc[g] * inverse).astype(BF16)
        for i in range(group):
            h = g * group + i
            for q in range(2):
                slot = row_slot(2 * side + q, z) - (2 if later else 0)
                at = pl.multiple_of(slot * part, part)
                src = i * rows + q * part
                out_ref[pl.ds(at, part), h * HEAD_DIM : (h + 1) * HEAD_DIM] = res[src : src + part]
    if not later:
        for f in fetches:
            f.wait()


def attention(page_len, doc_lengths, page_table, queries, kv_heads, got=(), weight=None, kv=None):
    later = kv is not None
    keys = queries.shape[0]
    rows = keys // 2
    group = queries.shape[1] // HEAD_DIM // kv_heads
    total = kv.shape[1] if later else len(got) * keys
    width = kv_heads * HEAD_DIM
    blocks = min(total // keys, total // 2 // keys + 1)
    out = [jax.ShapeDtypeStruct((rows, queries.shape[1]), BF16)]
    stat = pltpu.VMEM((kv_heads, group * rows, 128), F32)
    scratch = [
        pltpu.VMEM((kv_heads, group * rows, HEAD_DIM), BF16),
        pltpu.VMEM((blocks, kv_heads, group * rows, keys), F32),
        stat,
        stat,
        stat,
    ]
    near, specs = (queries, kv), None
    if not later:
        out.append(jax.ShapeDtypeStruct((2, total, width), BF16))
        out.append(jax.ShapeDtypeStruct(weight.shape, weight.dtype))
        scratch.insert(0, pltpu.SMEM((page_table.shape[0],), jnp.int32))
        scratch.append(pltpu.SemaphoreType.DMA((4,)))
        near = (queries, *got, in_hbm(weight))
        specs = [VMEM_SPEC] * (1 + len(got)) + [HBM_SPEC]
    return one_step(
        functools.partial(attention_kernel, page_len, later),
        "attention",
        out,
        (Far(doc_lengths, pltpu.SMEM), Far(page_table, pltpu.SMEM)),
        near,
        specs=specs,
        scratch=scratch,
        cost=((0 if later else 1280) * 1280 * group * rows * 128, 0 if later else 4 << 20, 0),
        room=5 * MIB + 4 * kv_heads * group * rows * keys * blocks,
    )


def fetch_kernel(pieces, *refs):
    *given, sem = refs
    given = given[1:]
    count = len(given) // 2
    copies = []
    for k in range(count):
        depth = given[k].shape[0] // pieces
        for i in range(pieces):
            here = slice(i * depth, (i + 1) * depth)
            copies.append(
                pltpu.make_async_copy(
                    given[k].at[here], given[count + k].at[here], sem.at[k * pieces + i]
                )
            )
    for c in copies:
        c.start()
    for c in copies:
        c.wait()


def fetch(after, *weights):
    return pl.pallas_call(
        functools.partial(fetch_kernel, 4),
        out_shape=tuple(jax.ShapeDtypeStruct(w.shape, w.dtype) for w in weights),
        in_specs=[ANY_SPEC] + [HBM_SPEC] * len(weights),
        out_specs=(VMEM_SPEC,) * len(weights),
        scratch_shapes=[pltpu.SemaphoreType.DMA((4 * len(weights),))],
        compiler_params=pltpu.CompilerParams(vmem_limit_bytes=1 * MIB),
        cost_estimate=pl.CostEstimate(
            flops=0, bytes_accessed=2 * sum(w.size for w in weights), transcendentals=0
        ),
        name="fetch",
    )(after, *(in_hbm(w) for w in weights))


def project_kernel(start, tile, side, att_ref, mix_ref, wa_ref, wm_ref, *out):
    part = out[0].shape[0]
    mix = mix_ref[2 * part * side : 2 * part * (side + 1), :]
    for send_ref, keep_ref in zip(out[::2], out[1::2]):
        width = send_ref.shape[1]
        for j in range(0, width, tile):
            here, there = slice(j, j + tile), slice(start + j, start + j + tile)
            total = nn(att_ref[...], wa_ref[:, there]) + nn(mix, wm_ref[:, there])
            send_ref[:, here] = total[:part].astype(BF16)
            keep_ref[:, here] = total[part:]
        start += width


def project(side, att, mix, wa, wm, start, widths, tile):
    rows, depth = att.shape
    width = sum(widths)
    out_shape = []
    for w in widths:
        out_shape.append(jax.ShapeDtypeStruct((rows // 2, w), BF16))
        out_shape.append(jax.ShapeDtypeStruct((rows // 2, w), F32))
    return pl.pallas_call(
        functools.partial(project_kernel, start, tile, side),
        out_shape=tuple(out_shape),
        in_specs=[VMEM_SPEC] * 4,
        out_specs=(VMEM_SPEC,) * len(out_shape),
        compiler_params=pltpu.CompilerParams(vmem_limit_bytes=4 * MIB),
        cost_estimate=pl.CostEstimate(
            flops=(1 - side) * 4 * rows * depth * width,
            bytes_accessed=(1 - side) * 6 * rows * width,
            transcendentals=0,
        ),
        name="project",
    )(att, mix, wa, wm)


def shards(
    n_ctx,
    n_tp,
    queries,
    key_pages,
    value_pages,
    mixer_input,
    state_write,
    state_read,
    log_decay,
    skip_gain,
    doc_lengths,
    page_table,
    attention_weight,
    mixer_weight,
):
    tok_rows = queries.shape[0]
    page_len = key_pages.shape[1]
    chips = n_ctx // 2

    def between_chips(a, j):
        return lax.ppermute(a, "ctx", [(i, i ^ (2 * j)) for i in range(n_ctx)])

    def other_core(a):
        return lax.ppermute(a, "ctx", [(i, i ^ 1) for i in range(n_ctx)])

    width = key_pages.shape[2]
    kv = jnp.stack([key_pages.reshape(-1, width), value_pages.reshape(-1, width)])
    kv, mixer_input = lax.optimization_barrier((kv, mixer_input))
    far = [kv] + [between_chips(kv, j) for j in range(1, chips)]

    base, st, eg = mixer_local(
        doc_lengths, skip_gain, mixer_input, state_write, state_read, log_decay
    )
    st_other = other_core(st)
    chip_state = compose(st, st_other)
    near_weight, near_queries, near_read = fetch(
        st, attention_weight, queries, state_read
    )
    far_states = [between_chips(chip_state, j) for j in range(1, chips)]

    far[1:], near_queries = lax.optimization_barrier((far[1:], near_queries))
    got = []
    for a in far:
        got += [a, other_core(a)]
    place = (page_len, doc_lengths, page_table, near_queries, width // HEAD_DIM)
    att, kv, far_weight = attention(*place, got, mixer_weight)
    *far_states, att = lax.optimization_barrier((*far_states, att))
    got_states = []
    for a in far_states:
        got_states += [a, other_core(a)]
    mix = finish(base, near_read, eg, st_other, got_states)

    part = tok_rows // n_tp
    columns = attention_weight.shape[1]
    widths = [share * columns // 8 for share in SHARES]
    weights = (near_weight, far_weight)

    def neighbour(a):
        return lax.ppermute(a, "tp", [(i, i ^ 1) for i in range(n_tp)])

    def across(a):
        return lax.ppermute(a, "tp", [(i, i ^ 2) for i in range(n_tp)])

    sums = list(project(0, att, mix, *weights, 0, widths[:1], 256))
    att, sums[0] = lax.optimization_barrier((att, sums[0]))
    sums += project(0, att, mix, *weights, widths[0], widths[1:], 256)
    kv, sums[2] = lax.optimization_barrier((kv, sums[2]))
    near_other = [neighbour(a) for a in sums[::2]]
    last, order = [], None
    for k, keep in enumerate(sums[1::2]):
        if order is not None:
            near_other[k], order = lax.optimization_barrier((near_other[k], order))
        if k == 2:
            near_other[k], last[1] = lax.optimization_barrier((near_other[k], last[1]))
        order = (keep + near_other[k].astype(F32)).astype(BF16)
        if k == 0:
            kv, order = lax.optimization_barrier((kv, order))
        last.append(across(order))
    (later,) = attention(*place, kv=kv)
    own_widths = (columns // 1,) * 1
    sums = project(1, later, mix, *weights, 0, own_widths, 256)
    near_own = [neighbour(a) for a in sums[::2]]
    near_own = near_own[0] if 1 == 1 else jnp.concatenate(near_own, axis=1)
    keep_own = sums[1] if 1 == 1 else jnp.concatenate(sums[1::2], axis=1)
    pieces, at = [], 0
    for a in last:
        here = slice(at, at + a.shape[1])
        own = keep_own[:, here] + near_own[:, here].astype(F32) + a.astype(F32)
        pieces.append(own.astype(BF16))
        at += a.shape[1]
    return jnp.concatenate(pieces, axis=1)


def solution(mesh):
    placed = (
        P("ctx", "tp"),
        P("ctx", None, "tp"),
        P("ctx", None, "tp"),
        P("ctx", "tp"),
        P("ctx", "tp"),
        P("ctx", "tp"),
        P("tp", "ctx"),
        P("tp"),
        P(),
        P(),
        P("tp", None),
        P("tp", None),
    )
    return jax.shard_map(
        functools.partial(shards, mesh.shape["ctx"], mesh.shape["tp"]),
        mesh=mesh,
        in_specs=placed,
        out_specs=P(("ctx", "tp"), None),
        check_vma=False,
    )
```

```python
import functools

import jax
import jax.numpy as jnp
from jax import lax
from jax.experimental import pallas as pl
from jax.experimental.pallas import tpu as pltpu
from jax.sharding import PartitionSpec as P

HEAD_DIM = 128
SSM_HEAD_DIM = 128
STATE = 128
LOG2E = 1.4426950408889634
LOW = -1e30
SHARES = (2, 2, 4)
F32 = jnp.float32
BF16 = jnp.bfloat16

MIB = 1 << 20
VMEM_SPEC = pl.BlockSpec(memory_space=pltpu.VMEM)
ANY_SPEC = pl.BlockSpec(memory_space=pl.ANY)
HBM_SPEC = pl.BlockSpec(memory_space=pltpu.HBM)


def in_hbm(a):
    return pltpu.with_memory_space_constraint(a, pltpu.HBM)


class Far:
    def __init__(self, array, space=pltpu.VMEM, lanes=None):
        self.array, self.lanes = array, lanes
        shape = array.shape if lanes is None else (array.shape[0], lanes.stop - lanes.start)
        self.scratch = space(shape, array.dtype)


def one_step(kernel, name, out_shape, far, near, scratch=(), cost=(0, 0, 0), room=6 * MIB, specs=None):
    flops, moved, exps = cost

    def body(*refs):
        given, refs = refs[: len(far)], refs[len(far) :]
        rest, held, sem = refs[: -len(far) - 1], refs[-len(far) - 1 : -1], refs[-1]
        copies = []
        for i, (f, src, dst) in enumerate(zip(far, given, held)):
            src = src if f.lanes is None else src.at[:, f.lanes]
            copies.append(pltpu.make_async_copy(src, dst, sem.at[i]))
        for c in copies:
            c.start()
        for c in copies:
            c.wait()
        kernel(*held, *rest)

    return pl.pallas_call(
        body,
        out_shape=tuple(out_shape),
        in_specs=[HBM_SPEC] * len(far) + (specs or [VMEM_SPEC] * len(near)),
        out_specs=(VMEM_SPEC,) * len(out_shape),
        scratch_shapes=[
            *scratch,
            *(f.scratch for f in far),
            pltpu.SemaphoreType.DMA((max(len(far), 1),)),
        ],
        compiler_params=pltpu.CompilerParams(vmem_limit_bytes=room),
        cost_estimate=pl.CostEstimate(flops=flops, bytes_accessed=moved, transcendentals=exps),
        name=name,
    )(*(in_hbm(f.array) for f in far), *near)


def doc_ends_of(len_ref):
    ends, total = [], 0
    for i in range(len_ref.shape[0]):
        total = total + len_ref[i]
        ends.append(total)
    return ends


def doc_start(pos, ends):
    start = jnp.zeros_like(pos)
    for end in ends:
        start = jnp.where(pos >= end, end, start)
    return start


def row_slot(part, z):
    return 3 - (part ^ z)


def nt(a, b):
    return lax.dot_general(a, b, (((1,), (1,)), ((), ())), preferred_element_type=F32)


def nn(a, b):
    return lax.dot_general(a, b, (((1,), (0,)), ((), ())), preferred_element_type=F32)


def mixer_kernel(len_ref, skip_ref, x_ref, w_ref, r_ref, ld_ref, base_ref, st_ref, eg_ref):
    me = lax.axis_index("ctx")
    heads, rows = ld_ref.shape
    groups = w_ref.shape[1] // STATE
    per_group = heads // groups
    half = heads // 2
    first = me * rows
    ends = doc_ends_of(len_ref)
    ds = ld_ref[...]
    lane = lax.broadcasted_iota(jnp.int32, ds.shape, 1)
    shift = 1
    while shift < rows:
        ds = ds + jnp.where(lane >= shift, pltpu.roll(ds, shift, 1), 0.0)
        shift *= 2
    col = ds.T
    t_pos = first + lax.broadcasted_iota(jnp.int32, (rows, 1), 0)
    t_start = doc_start(t_pos, ends)
    s_pos = first + lax.broadcasted_iota(jnp.int32, (1, rows), 1)
    last = first + rows - 1
    last_start = doc_start(jnp.full((1, 1), last, jnp.int32), ends)
    visible = (s_pos <= t_pos) & (s_pos >= t_start)
    bias = jnp.where(visible, 0.0, LOW)
    eg_ref[...] = jnp.where(t_start < first, jnp.exp(col), 0.0)
    total = ds[:, rows - 1 : rows]
    end_weight = jnp.where(s_pos >= last_start, jnp.exp(total - ds), 0.0)
    gain = jnp.where(last_start < first, jnp.exp(total), 0.0)
    gain = jnp.broadcast_to(gain, (heads, SSM_HEAD_DIM)).astype(BF16)
    pad = jnp.zeros((st_ref.shape[1] - half * STATE - half, SSM_HEAD_DIM), BF16)
    for c in range(2):
        st_ref[c, half * STATE :, :] = jnp.concatenate(
            [gain[c * half : (c + 1) * half].astype(F32), pad.astype(F32)], axis=0
        ).astype(BF16)
    for g in range(groups):
        cols = slice(g * STATE, (g + 1) * STATE)
        write, read = w_ref[:, cols], r_ref[:, cols]
        inner = nt(read, write)
        write_t = write.astype(F32).T
        for h in range(g * per_group, (g + 1) * per_group):
            hc = slice(h * SSM_HEAD_DIM, (h + 1) * SSM_HEAD_DIM)
            x = x_ref[:, hc]
            decay = jnp.exp((col[:, h : h + 1] - ds[h : h + 1, :]) + bias)
            mixing = (decay * inner).astype(BF16)
            base_ref[:, hc] = nn(mixing, x) + skip_ref[h] * x.astype(F32)
            end_write = (write_t * end_weight[h : h + 1, :]).astype(BF16)
            c, i = divmod(h, half)
            st_ref[c, i * STATE : (i + 1) * STATE, :] = nn(end_write, x).astype(BF16)


def mixer_local(doc_lengths, skip_gain, x, w, r, ld):
    heads, rows = ld.shape
    half = heads // 2
    return one_step(
        mixer_kernel,
        "mixer_local",
        (
            jax.ShapeDtypeStruct(x.shape, F32),
            jax.ShapeDtypeStruct((2, half * STATE + 16, SSM_HEAD_DIM), BF16),
            jax.ShapeDtypeStruct((rows, heads), F32),
        ),
        (Far(doc_lengths, pltpu.SMEM), Far(skip_gain, pltpu.SMEM), Far(x), Far(w), Far(r), Far(ld)),
        (),
    )


def compose_kernel(mine_ref, other_ref, out_ref):
    core = lax.axis_index("ctx") & 1
    state_rows = out_ref.shape[0] - 16
    half = state_rows // STATE
    a, b = mine_ref[core].astype(F32), other_ref[core].astype(F32)
    first = jnp.where(core == 0, a, b)
    second = jnp.where(core == 0, b, a)
    for i in range(half):
        rows = slice(i * STATE, (i + 1) * STATE)
        gain = second[state_rows + i : state_rows + i + 1]
        out_ref[rows, :] = (gain * first[rows] + second[rows]).astype(BF16)
    out_ref[state_rows:, :] = (first[state_rows:] * second[state_rows:]).astype(BF16)


def compose(mine, other):
    return pl.pallas_call(
        compose_kernel,
        out_shape=jax.ShapeDtypeStruct(mine.shape[1:], BF16),
        in_specs=[VMEM_SPEC] * 2,
        out_specs=VMEM_SPEC,
        compiler_params=pltpu.CompilerParams(vmem_limit_bytes=4 * MIB),
        cost_estimate=pl.CostEstimate(flops=0, bytes_accessed=0, transcendentals=0),
        name="compose",
    )(mine, other)


def finish_kernel(r_ref, base_ref, eg_ref, st_ref, *refs):
    *got, out_ref, held, carry = refs
    me = lax.axis_index("ctx")
    core, chip = me & 1, me // 2
    z = lax.axis_index("tp")
    rows = base_ref.shape[0]
    part = rows // 4
    state_rows = st_ref.shape[1] - 16
    half = state_rows // STATE
    groups = r_ref.shape[1] // STATE
    heads = 2 * half
    per_group = heads // groups
    for j in range(1, held.shape[0]):
        held[chip ^ j, core] = got[2 * j - 2][...]
        held[chip ^ j, core ^ 1] = got[2 * j - 1][...]
    carry[...] = jnp.zeros_like(carry)

    def where(h):
        c, i = divmod(h, half)
        return c, slice(i * STATE, (i + 1) * STATE), slice(state_rows + i, state_rows + i + 1)

    def one(k, _):
        for h in range(heads):
            c, hs, gs = where(h)
            carry[h] = held[k, c, gs, :].astype(F32) * carry[h] + held[k, c, hs, :].astype(F32)
        return 0

    lax.fori_loop(0, chip, one, 0)

    @pl.when(core == 1)
    def _():
        for h in range(heads):
            c, hs, gs = where(h)
            carry[h] = st_ref[c, gs, :].astype(F32) * carry[h] + st_ref[c, hs, :].astype(F32)

    for h in range(heads):
        hc = slice(h * SSM_HEAD_DIM, (h + 1) * SSM_HEAD_DIM)
        g = h // per_group
        inter = nn(r_ref[:, g * STATE : (g + 1) * STATE], carry[h].astype(BF16))
        res = (base_ref[:, hc] + eg_ref[:, h : h + 1] * inter).astype(BF16)
        for q in range(4):
            at = pl.multiple_of(row_slot(q, z) * part, part)
            out_ref[pl.ds(at, part), hc] = res[q * part : (q + 1) * part]


def finish(base, r, eg, st_other, got):
    chips = len(got) // 2 + 1
    heads = base.shape[1] // SSM_HEAD_DIM
    return one_step(
        finish_kernel,
        "finish",
        (jax.ShapeDtypeStruct(base.shape, BF16),),
        (),
        (r, base, eg, st_other, *got),
        scratch=[
            pltpu.VMEM((chips, 2) + got[0].shape, BF16),
            pltpu.VMEM((heads, STATE, SSM_HEAD_DIM), F32),
        ],
        room=(4 + chips) * MIB,
    )[0]


def attention_kernel(page_len, later, len_ref, table_ref, q_ref, *refs):
    if later:
        kv, out_ref, qs, sc, mx, ls, acc = refs
    else:
        *got, out_ref, kv, inv, qs, sc, mx, ls, acc = refs
    me = lax.axis_index("ctx")
    z = lax.axis_index("tp")
    keys = q_ref.shape[0]
    rows = keys // 2
    part = rows // 2
    kv_heads = kv.shape[2] // HEAD_DIM
    group = q_ref.shape[1] // HEAD_DIM // kv_heads
    stacked = group * rows
    ends = doc_ends_of(len_ref)
    start0 = 0
    for end in ends:
        start0 = jnp.where(me * keys >= end, end, start0)
    low_block = start0 // keys
    side = z // 2 if later else 1 - z // 2

    if not later:

        def invert(l, _):
            inv[table_ref[l]] = l
            return 0

        lax.fori_loop(0, table_ref.shape[0], invert, 0, unroll=8)
        for j, ref in enumerate(got):
            pages = ref.shape[1] // page_len
            for slot in range(pages):
                page = inv[(me ^ j) * pages + slot]
                there = pl.ds(pl.multiple_of(page * page_len, page_len), page_len)
                here = slice(slot * page_len, (slot + 1) * page_len)
                for i in range(2):
                    kv[i, there, :] = ref[i, here, :]

    here = pl.ds(pl.multiple_of(side * rows, rows), rows)
    for h in range(kv_heads * group):
        g, i = divmod(h, group)
        qs[g, i * rows : (i + 1) * rows, :] = q_ref[here, h * HEAD_DIM : (h + 1) * HEAD_DIM]
    row = lax.rem(lax.broadcasted_iota(jnp.int32, (min(stacked, 256), 1), 0), rows)
    t_pos = me * keys + side * rows + row
    t_start = doc_start(t_pos, ends)
    scale = LOG2E * HEAD_DIM ** (-0.5)

    def lanes(g):
        return slice(g * HEAD_DIM, (g + 1) * HEAD_DIM)

    unit = min(stacked, 256)
    units = [(g, slice(r, r + unit)) for g in range(kv_heads) for r in range(0, stacked, unit)]

    def scores(block, own):
        at = pl.ds(pl.multiple_of(block * keys, keys), keys)
        u_pos = block * keys + lax.broadcasted_iota(jnp.int32, (1, keys), 1)
        shown = u_pos >= t_start
        if own:
            shown = shown & (u_pos <= t_pos)
        for g, r in units:
            s = nt(qs[g, r, :], kv[0, at, lanes(g)])
            s = jnp.where(shown, s * scale, LOW)
            sc[block - low_block, g, r, :] = s
            top = s[:, :128]
            for k in range(128, keys, 128):
                top = jnp.maximum(top, s[:, k : k + 128])
            mx[g, r, :] = top if own else jnp.maximum(mx[g, r, :], top)

    scores(me, True)

    def earlier(block, _):
        scores(block, False)
        return 0

    lax.fori_loop(low_block, me, earlier, 0)
    for g in range(kv_heads):
        mx[g] = jnp.broadcast_to(jnp.max(mx[g], axis=1, keepdims=True), (stacked, 128))

    def weigh(block, own):
        at = pl.ds(pl.multiple_of(block * keys, keys), keys)
        for g, r in units:
            m = mx[g, r, :]
            total, pieces = None, []
            for k in range(0, keys, 128):
                w = jnp.exp2(sc[block - low_block, g, r, k : k + 128] - m)
                total = w if total is None else total + w
                pieces.append(w.astype(BF16))
            term = nn(jnp.concatenate(pieces, axis=1), kv[1, at, lanes(g)])
            ls[g, r, :] = total if own else ls[g, r, :] + total
            acc[g, r, :] = term if own else acc[g, r, :] + term

    weigh(me, True)

    def weigh_earlier(block, _):
        weigh(block, False)
        return 0

    lax.fori_loop(low_block, me, weigh_earlier, 0)
    for g in range(kv_heads):
        inverse = 1.0 / jnp.sum(ls[g], axis=1, keepdims=True)
        res = (acc[g] * inverse).astype(BF16)
        for i in range(group):
            h = g * group + i
            for q in range(2):
                slot = row_slot(2 * side + q, z) - (2 if later else 0)
                at = pl.multiple_of(slot * part, part)
                src = i * rows + q * part
                out_ref[pl.ds(at, part), h * HEAD_DIM : (h + 1) * HEAD_DIM] = res[src : src + part]


def attention(page_len, doc_lengths, page_table, queries, kv_heads, got=(), kv=None):
    later = kv is not None
    keys = queries.shape[0]
    rows = keys // 2
    group = queries.shape[1] // HEAD_DIM // kv_heads
    total = kv.shape[1] if later else len(got) * keys
    width = kv_heads * HEAD_DIM
    blocks = min(total // keys, total // 2 // keys + 1)
    out = [jax.ShapeDtypeStruct((rows, queries.shape[1]), BF16)]
    stat = pltpu.VMEM((kv_heads, group * rows, 128), F32)
    scratch = [
        pltpu.VMEM((kv_heads, group * rows, HEAD_DIM), BF16),
        pltpu.VMEM((blocks, kv_heads, group * rows, keys), F32),
        stat,
        stat,
        stat,
    ]
    near = (queries, kv)
    if not later:
        out.append(jax.ShapeDtypeStruct((2, total, width), BF16))
        scratch.insert(0, pltpu.SMEM((page_table.shape[0],), jnp.int32))
        near = (queries, *got)
    return one_step(
        functools.partial(attention_kernel, page_len, later),
        "attention",
        out,
        (Far(doc_lengths, pltpu.SMEM), Far(page_table, pltpu.SMEM)),
        near,
        scratch=scratch,
        cost=((0 if later else 1280) * 1280 * group * rows * 128, 0 if later else 4 << 20, 0),
        room=5 * MIB + 4 * kv_heads * group * rows * keys * blocks,
    )


def fetch_kernel(pieces, *refs):
    *given, sem = refs
    given = given[1:]
    count = len(given) // 2
    copies = []
    for k in range(count):
        depth = given[k].shape[0] // pieces
        for i in range(pieces):
            here = slice(i * depth, (i + 1) * depth)
            copies.append(
                pltpu.make_async_copy(
                    given[k].at[here], given[count + k].at[here], sem.at[k * pieces + i]
                )
            )
    for c in copies:
        c.start()
    for c in copies:
        c.wait()


def fetch(after, *weights):
    return pl.pallas_call(
        functools.partial(fetch_kernel, 4),
        out_shape=tuple(jax.ShapeDtypeStruct(w.shape, w.dtype) for w in weights),
        in_specs=[ANY_SPEC] + [HBM_SPEC] * len(weights),
        out_specs=(VMEM_SPEC,) * len(weights),
        scratch_shapes=[pltpu.SemaphoreType.DMA((4 * len(weights),))],
        compiler_params=pltpu.CompilerParams(vmem_limit_bytes=1 * MIB),
        cost_estimate=pl.CostEstimate(
            flops=0, bytes_accessed=2 * sum(w.size for w in weights), transcendentals=0
        ),
        name="fetch",
    )(after, *(in_hbm(w) for w in weights))


def project_kernel(start, tile, side, att_ref, mix_ref, wa_ref, wm_ref, *out):
    part = out[0].shape[0]
    mix = mix_ref[2 * part * side : 2 * part * (side + 1), :]
    for send_ref, keep_ref in zip(out[::2], out[1::2]):
        width = send_ref.shape[1]
        for j in range(0, width, tile):
            here, there = slice(j, j + tile), slice(start + j, start + j + tile)
            total = nn(att_ref[...], wa_ref[:, there]) + nn(mix, wm_ref[:, there])
            send_ref[:, here] = total[:part].astype(BF16)
            keep_ref[:, here] = total[part:]
        start += width


def project(side, att, mix, wa, wm, start, widths, tile):
    rows, depth = att.shape
    width = sum(widths)
    out_shape = []
    for w in widths:
        out_shape.append(jax.ShapeDtypeStruct((rows // 2, w), BF16))
        out_shape.append(jax.ShapeDtypeStruct((rows // 2, w), F32))
    return pl.pallas_call(
        functools.partial(project_kernel, start, tile, side),
        out_shape=tuple(out_shape),
        in_specs=[VMEM_SPEC] * 4,
        out_specs=(VMEM_SPEC,) * len(out_shape),
        compiler_params=pltpu.CompilerParams(vmem_limit_bytes=4 * MIB),
        cost_estimate=pl.CostEstimate(
            flops=(1 - side) * 4 * rows * depth * width,
            bytes_accessed=(1 - side) * 6 * rows * width,
            transcendentals=0,
        ),
        name="project",
    )(att, mix, wa, wm)


def pack_kernel(key_ref, value_ref, out_ref, sem):
    copies = [
        pltpu.make_async_copy(ref, out_ref.at[i], sem.at[i])
        for i, ref in enumerate((key_ref, value_ref))
    ]
    for c in copies:
        c.start()
    for c in copies:
        c.wait()


def pack(keys, values):
    return pl.pallas_call(
        pack_kernel,
        out_shape=jax.ShapeDtypeStruct((2,) + keys.shape, keys.dtype),
        in_specs=[HBM_SPEC] * 2,
        out_specs=VMEM_SPEC,
        scratch_shapes=[pltpu.SemaphoreType.DMA((2,))],
        compiler_params=pltpu.CompilerParams(vmem_limit_bytes=1 * MIB),
        cost_estimate=pl.CostEstimate(flops=0, bytes_accessed=0, transcendentals=0),
        name="pack",
    )(in_hbm(keys), in_hbm(values))


def assemble_kernel(keep_ref, near_ref, *refs):
    *last, out_ref, held, sem = refs
    at, copies = 0, []
    for ref in last:
        here = slice(at, at + ref.shape[1])
        total = keep_ref[:, here] + near_ref[:, here].astype(F32) + ref[...].astype(F32)
        held[:, here] = total.astype(BF16)
        copies.append(
            pltpu.make_async_copy(held.at[:, here], out_ref.at[:, here], sem.at[len(copies)])
        )
        copies[-1].start()
        at += ref.shape[1]
    for c in copies:
        c.wait()


def assemble(keep, near, last):
    return pl.pallas_call(
        assemble_kernel,
        out_shape=jax.ShapeDtypeStruct(keep.shape, BF16),
        in_specs=[VMEM_SPEC] * (2 + len(last)),
        out_specs=HBM_SPEC,
        scratch_shapes=[pltpu.VMEM(keep.shape, BF16), pltpu.SemaphoreType.DMA((len(last),))],
        compiler_params=pltpu.CompilerParams(vmem_limit_bytes=2 * MIB),
        cost_estimate=pl.CostEstimate(flops=0, bytes_accessed=0, transcendentals=0),
        name="assemble",
    )(keep, near, *last)


def shards(
    n_ctx,
    n_tp,
    queries,
    key_pages,
    value_pages,
    mixer_input,
    state_write,
    state_read,
    log_decay,
    skip_gain,
    doc_lengths,
    page_table,
    attention_weight,
    mixer_weight,
):
    tok_rows = queries.shape[0]
    page_len = key_pages.shape[1]
    chips = n_ctx // 2

    def between_chips(a, j):
        return lax.ppermute(a, "ctx", [(i, i ^ (2 * j)) for i in range(n_ctx)])

    def other_core(a):
        return lax.ppermute(a, "ctx", [(i, i ^ 1) for i in range(n_ctx)])

    width = key_pages.shape[2]
    kv = pack(key_pages.reshape(-1, width), value_pages.reshape(-1, width))
    kv, mixer_input = lax.optimization_barrier((kv, mixer_input))
    far = [kv] + [between_chips(kv, j) for j in range(1, chips)]

    base, st, eg = mixer_local(
        doc_lengths, skip_gain, mixer_input, state_write, state_read, log_decay
    )
    st_other = other_core(st)
    chip_state = compose(st, st_other)
    near_weight, far_weight, near_queries, near_read = fetch(
        st, attention_weight, mixer_weight, queries, state_read
    )
    far_states = [between_chips(chip_state, j) for j in range(1, chips)]

    far[1:], near_queries = lax.optimization_barrier((far[1:], near_queries))
    got = []
    for a in far:
        got += [a, other_core(a)]
    place = (page_len, doc_lengths, page_table, near_queries, width // HEAD_DIM)
    att, kv = attention(*place, got)
    *far_states, att = lax.optimization_barrier((*far_states, att))
    got_states = []
    for a in far_states:
        got_states += [a, other_core(a)]
    mix = finish(base, near_read, eg, st_other, got_states)

    part = tok_rows // n_tp
    columns = attention_weight.shape[1]
    widths = [share * columns // 8 for share in SHARES]
    weights = (near_weight, far_weight)

    def neighbour(a):
        return lax.ppermute(a, "tp", [(i, i ^ 1) for i in range(n_tp)])

    def across(a):
        return lax.ppermute(a, "tp", [(i, i ^ 2) for i in range(n_tp)])

    sums = list(project(0, att, mix, *weights, 0, widths[:1], 256))
    att, sums[0] = lax.optimization_barrier((att, sums[0]))
    sums += project(0, att, mix, *weights, widths[0], widths[1:], 256)
    kv, sums[2] = lax.optimization_barrier((kv, sums[2]))
    near_other = [neighbour(a) for a in sums[::2]]
    last, order = [], None
    for k, keep in enumerate(sums[1::2]):
        if order is not None:
            near_other[k], order = lax.optimization_barrier((near_other[k], order))
        if k == 2:
            near_other[k], last[0] = lax.optimization_barrier((near_other[k], last[0]))
        if k == 2:
            near_other[k], last[1] = lax.optimization_barrier((near_other[k], last[1]))
        order = (keep + near_other[k].astype(F32)).astype(BF16)
        if k == 0:
            kv, order = lax.optimization_barrier((kv, order))
        last.append(across(order))
    (later,) = attention(*place, kv=kv)
    send_own, keep_own = project(1, later, mix, *weights, 0, (columns,), 256)
    near_own = neighbour(send_own)
    return assemble(keep_own, near_own, last)


def solution(mesh):
    placed = (
        P("ctx", "tp"),
        P("ctx", None, "tp"),
        P("ctx", None, "tp"),
        P("ctx", "tp"),
        P("ctx", "tp"),
        P("ctx", "tp"),
        P("tp", "ctx"),
        P("tp"),
        P(),
        P(),
        P("tp", None),
        P("tp", None),
    )
    return jax.shard_map(
        functools.partial(shards, mesh.shape["ctx"], mesh.shape["tp"]),
        mesh=mesh,
        in_specs=placed,
        out_specs=P(("ctx", "tp"), None),
        check_vma=False,
    )
```

```python
import functools

import jax
import jax.numpy as jnp
from jax import lax
from jax.experimental import pallas as pl
from jax.experimental.pallas import tpu as pltpu
from jax.sharding import PartitionSpec as P

HEAD_DIM = 128
SSM_HEAD_DIM = 128
STATE = 128
LOG2E = 1.4426950408889634
LOW = -1e30
SHARES = (2, 2, 4)
F32 = jnp.float32
BF16 = jnp.bfloat16

MIB = 1 << 20
VMEM_SPEC = pl.BlockSpec(memory_space=pltpu.VMEM)
ANY_SPEC = pl.BlockSpec(memory_space=pl.ANY)
HBM_SPEC = pl.BlockSpec(memory_space=pltpu.HBM)


def in_hbm(a):
    return pltpu.with_memory_space_constraint(a, pltpu.HBM)


class Far:
    def __init__(self, array, space=pltpu.VMEM, lanes=None):
        self.array, self.lanes = array, lanes
        shape = array.shape if lanes is None else (array.shape[0], lanes.stop - lanes.start)
        self.scratch = space(shape, array.dtype)


def one_step(kernel, name, out_shape, far, near, scratch=(), cost=(0, 0, 0), room=6 * MIB, specs=None):
    flops, moved, exps = cost

    def body(*refs):
        given, refs = refs[: len(far)], refs[len(far) :]
        rest, held, sem = refs[: -len(far) - 1], refs[-len(far) - 1 : -1], refs[-1]
        copies = []
        for i, (f, src, dst) in enumerate(zip(far, given, held)):
            src = src if f.lanes is None else src.at[:, f.lanes]
            copies.append(pltpu.make_async_copy(src, dst, sem.at[i]))
        for c in copies:
            c.start()
        for c in copies:
            c.wait()
        kernel(*held, *rest)

    return pl.pallas_call(
        body,
        out_shape=tuple(out_shape),
        in_specs=[HBM_SPEC] * len(far) + (specs or [VMEM_SPEC] * len(near)),
        out_specs=(VMEM_SPEC,) * len(out_shape),
        scratch_shapes=[
            *scratch,
            *(f.scratch for f in far),
            pltpu.SemaphoreType.DMA((max(len(far), 1),)),
        ],
        compiler_params=pltpu.CompilerParams(vmem_limit_bytes=room),
        cost_estimate=pl.CostEstimate(flops=flops, bytes_accessed=moved, transcendentals=exps),
        name=name,
    )(*(in_hbm(f.array) for f in far), *near)


def doc_ends_of(len_ref):
    ends, total = [], 0
    for i in range(len_ref.shape[0]):
        total = total + len_ref[i]
        ends.append(total)
    return ends


def doc_start(pos, ends):
    start = jnp.zeros_like(pos)
    for end in ends:
        start = jnp.where(pos >= end, end, start)
    return start


def row_slot(part, z):
    return 3 - (part ^ z)


def nt(a, b):
    return lax.dot_general(a, b, (((1,), (1,)), ((), ())), preferred_element_type=F32)


def nn(a, b):
    return lax.dot_general(a, b, (((1,), (0,)), ((), ())), preferred_element_type=F32)


def mixer_kernel(len_ref, skip_ref, x_ref, w_ref, r_ref, ld_ref, base_ref, st_ref, eg_ref):
    me = lax.axis_index("ctx")
    heads, rows = ld_ref.shape
    groups = w_ref.shape[1] // STATE
    per_group = heads // groups
    half = heads // 2
    first = me * rows
    ends = doc_ends_of(len_ref)
    ds = ld_ref[...]
    lane = lax.broadcasted_iota(jnp.int32, ds.shape, 1)
    shift = 1
    while shift < rows:
        ds = ds + jnp.where(lane >= shift, pltpu.roll(ds, shift, 1), 0.0)
        shift *= 2
    col = ds.T
    t_pos = first + lax.broadcasted_iota(jnp.int32, (rows, 1), 0)
    t_start = doc_start(t_pos, ends)
    s_pos = first + lax.broadcasted_iota(jnp.int32, (1, rows), 1)
    last = first + rows - 1
    last_start = doc_start(jnp.full((1, 1), last, jnp.int32), ends)
    visible = (s_pos <= t_pos) & (s_pos >= t_start)
    bias = jnp.where(visible, 0.0, LOW)
    eg_ref[...] = jnp.where(t_start < first, jnp.exp(col), 0.0)
    total = ds[:, rows - 1 : rows]
    end_weight = jnp.where(s_pos >= last_start, jnp.exp(total - ds), 0.0)
    gain = jnp.where(last_start < first, jnp.exp(total), 0.0)
    gain = jnp.broadcast_to(gain, (heads, SSM_HEAD_DIM)).astype(BF16)
    pad = jnp.zeros((st_ref.shape[1] - half * STATE - half, SSM_HEAD_DIM), BF16)
    for c in range(2):
        st_ref[c, half * STATE :, :] = jnp.concatenate(
            [gain[c * half : (c + 1) * half].astype(F32), pad.astype(F32)], axis=0
        ).astype(BF16)
    for g in range(groups):
        cols = slice(g * STATE, (g + 1) * STATE)
        write, read = w_ref[:, cols], r_ref[:, cols]
        inner = nt(read, write)
        write_t = write.astype(F32).T
        for h in range(g * per_group, (g + 1) * per_group):
            hc = slice(h * SSM_HEAD_DIM, (h + 1) * SSM_HEAD_DIM)
            x = x_ref[:, hc]
            decay = jnp.exp((col[:, h : h + 1] - ds[h : h + 1, :]) + bias)
            mixing = (decay * inner).astype(BF16)
            base_ref[:, hc] = nn(mixing, x) + skip_ref[h] * x.astype(F32)
            end_write = (write_t * end_weight[h : h + 1, :]).astype(BF16)
            c, i = divmod(h, half)
            st_ref[c, i * STATE : (i + 1) * STATE, :] = nn(end_write, x).astype(BF16)


def mixer_local(doc_lengths, skip_gain, x, w, r, ld):
    heads, rows = ld.shape
    half = heads // 2
    return one_step(
        mixer_kernel,
        "mixer_local",
        (
            jax.ShapeDtypeStruct(x.shape, F32),
            jax.ShapeDtypeStruct((2, half * STATE + 16, SSM_HEAD_DIM), BF16),
            jax.ShapeDtypeStruct((rows, heads), F32),
        ),
        (Far(doc_lengths, pltpu.SMEM), Far(skip_gain, pltpu.SMEM), Far(x), Far(w), Far(r), Far(ld)),
        (),
    )


def compose_kernel(mine_ref, low_ref, high_ref, out_ref):
    core = lax.axis_index("ctx") & 1
    state_rows = out_ref.shape[0] - 16
    half = state_rows // STATE
    a = mine_ref[core].astype(F32)
    b = jnp.where(core == 0, low_ref[...].astype(F32), high_ref[...].astype(F32))
    first = jnp.where(core == 0, a, b)
    second = jnp.where(core == 0, b, a)
    for i in range(half):
        rows = slice(i * STATE, (i + 1) * STATE)
        gain = second[state_rows + i : state_rows + i + 1]
        out_ref[rows, :] = (gain * first[rows] + second[rows]).astype(BF16)
    out_ref[state_rows:, :] = (first[state_rows:] * second[state_rows:]).astype(BF16)


def compose(mine, low, high):
    return pl.pallas_call(
        compose_kernel,
        out_shape=jax.ShapeDtypeStruct(mine.shape[1:], BF16),
        in_specs=[VMEM_SPEC] * 3,
        out_specs=VMEM_SPEC,
        compiler_params=pltpu.CompilerParams(vmem_limit_bytes=4 * MIB),
        cost_estimate=pl.CostEstimate(flops=0, bytes_accessed=0, transcendentals=0),
        name="compose",
    )(mine, low, high)


def finish_kernel(r_ref, base_ref, eg_ref, low_ref, high_ref, *refs):
    *got, out_ref, held, carry = refs
    me = lax.axis_index("ctx")
    core, chip = me & 1, me // 2
    z = lax.axis_index("tp")
    rows = base_ref.shape[0]
    part = rows // 4
    state_rows = low_ref.shape[0] - 16
    half = state_rows // STATE
    groups = r_ref.shape[1] // STATE
    heads = 2 * half
    per_group = heads // groups
    for j in range(1, held.shape[0]):
        held[chip ^ j, core] = got[2 * j - 2][...]
        held[chip ^ j, core ^ 1] = got[2 * j - 1][...]
    carry[...] = jnp.zeros_like(carry)

    def where(h):
        c, i = divmod(h, half)
        return c, slice(i * STATE, (i + 1) * STATE), slice(state_rows + i, state_rows + i + 1)

    def one(k, _):
        for h in range(heads):
            c, hs, gs = where(h)
            carry[h] = held[k, c, gs, :].astype(F32) * carry[h] + held[k, c, hs, :].astype(F32)
        return 0

    lax.fori_loop(0, chip, one, 0)

    @pl.when(core == 1)
    def _():
        for h in range(heads):
            c, hs, gs = where(h)
            ref = high_ref if c else low_ref
            carry[h] = ref[gs, :].astype(F32) * carry[h] + ref[hs, :].astype(F32)

    for h in range(heads):
        hc = slice(h * SSM_HEAD_DIM, (h + 1) * SSM_HEAD_DIM)
        g = h // per_group
        inter = nn(r_ref[:, g * STATE : (g + 1) * STATE], carry[h].astype(BF16))
        res = (base_ref[:, hc] + eg_ref[:, h : h + 1] * inter).astype(BF16)
        for q in range(4):
            at = pl.multiple_of(row_slot(q, z) * part, part)
            out_ref[pl.ds(at, part), hc] = res[q * part : (q + 1) * part]


def finish(base, r, eg, low, high, got):
    chips = len(got) // 2 + 1
    heads = base.shape[1] // SSM_HEAD_DIM
    return one_step(
        finish_kernel,
        "finish",
        (jax.ShapeDtypeStruct(base.shape, BF16),),
        (),
        (r, base, eg, low, high, *got),
        scratch=[
            pltpu.VMEM((chips, 2) + got[0].shape, BF16),
            pltpu.VMEM((heads, STATE, SSM_HEAD_DIM), F32),
        ],
        room=(4 + chips) * MIB,
    )[0]


def attention_kernel(page_len, later, len_ref, table_ref, q_ref, *refs):
    if later:
        kv, out_ref, qs, sc, mx, ls, acc = refs
    else:
        *got, out_ref, kv, inv, qs, sc, mx, ls, acc = refs
    me = lax.axis_index("ctx")
    z = lax.axis_index("tp")
    keys = q_ref.shape[0]
    rows = keys // 2
    part = rows // 2
    kv_heads = kv.shape[2] // HEAD_DIM
    group = q_ref.shape[1] // HEAD_DIM // kv_heads
    stacked = group * rows
    ends = doc_ends_of(len_ref)
    start0 = 0
    for end in ends:
        start0 = jnp.where(me * keys >= end, end, start0)
    low_block = start0 // keys
    side = z // 2 if later else 1 - z // 2

    if not later:

        def invert(l, _):
            inv[table_ref[l]] = l
            return 0

        lax.fori_loop(0, table_ref.shape[0], invert, 0, unroll=8)
        for j, ref in enumerate(got):
            pages = ref.shape[1] // page_len
            for slot in range(pages):
                page = inv[(me ^ j) * pages + slot]
                there = pl.ds(pl.multiple_of(page * page_len, page_len), page_len)
                here = slice(slot * page_len, (slot + 1) * page_len)
                for i in range(2):
                    kv[i, there, :] = ref[i, here, :]

    here = pl.ds(pl.multiple_of(side * rows, rows), rows)
    for h in range(kv_heads * group):
        g, i = divmod(h, group)
        qs[g, i * rows : (i + 1) * rows, :] = q_ref[here, h * HEAD_DIM : (h + 1) * HEAD_DIM]
    row = lax.rem(lax.broadcasted_iota(jnp.int32, (min(stacked, 256), 1), 0), rows)
    t_pos = me * keys + side * rows + row
    t_start = doc_start(t_pos, ends)
    scale = LOG2E * HEAD_DIM ** (-0.5)

    def lanes(g):
        return slice(g * HEAD_DIM, (g + 1) * HEAD_DIM)

    unit = min(stacked, 256)
    units = [(g, slice(r, r + unit)) for g in range(kv_heads) for r in range(0, stacked, unit)]

    def scores(block, own):
        at = pl.ds(pl.multiple_of(block * keys, keys), keys)
        u_pos = block * keys + lax.broadcasted_iota(jnp.int32, (1, keys), 1)
        shown = u_pos >= t_start
        if own:
            shown = shown & (u_pos <= t_pos)
        for g, r in units:
            s = nt(qs[g, r, :], kv[0, at, lanes(g)])
            s = jnp.where(shown, s * scale, LOW)
            sc[block - low_block, g, r, :] = s
            top = s[:, :128]
            for k in range(128, keys, 128):
                top = jnp.maximum(top, s[:, k : k + 128])
            mx[g, r, :] = top if own else jnp.maximum(mx[g, r, :], top)

    scores(me, True)

    def earlier(block, _):
        scores(block, False)
        return 0

    lax.fori_loop(low_block, me, earlier, 0)
    for g in range(kv_heads):
        mx[g] = jnp.broadcast_to(jnp.max(mx[g], axis=1, keepdims=True), (stacked, 128))

    def weigh(block, own):
        at = pl.ds(pl.multiple_of(block * keys, keys), keys)
        for g, r in units:
            m = mx[g, r, :]
            total, pieces = None, []
            for k in range(0, keys, 128):
                w = jnp.exp2(sc[block - low_block, g, r, k : k + 128] - m)
                total = w if total is None else total + w
                pieces.append(w.astype(BF16))
            term = nn(jnp.concatenate(pieces, axis=1), kv[1, at, lanes(g)])
            ls[g, r, :] = total if own else ls[g, r, :] + total
            acc[g, r, :] = term if own else acc[g, r, :] + term

    weigh(me, True)

    def weigh_earlier(block, _):
        weigh(block, False)
        return 0

    lax.fori_loop(low_block, me, weigh_earlier, 0)
    for g in range(kv_heads):
        inverse = 1.0 / jnp.sum(ls[g], axis=1, keepdims=True)
        res = (acc[g] * inverse).astype(BF16)
        for i in range(group):
            h = g * group + i
            for q in range(2):
                slot = row_slot(2 * side + q, z) - (2 if later else 0)
                at = pl.multiple_of(slot * part, part)
                src = i * rows + q * part
                out_ref[pl.ds(at, part), h * HEAD_DIM : (h + 1) * HEAD_DIM] = res[src : src + part]


def attention(page_len, doc_lengths, page_table, queries, kv_heads, got=(), kv=None):
    later = kv is not None
    keys = queries.shape[0]
    rows = keys // 2
    group = queries.shape[1] // HEAD_DIM // kv_heads
    total = kv.shape[1] if later else len(got) * keys
    width = kv_heads * HEAD_DIM
    blocks = min(total // keys, total // 2 // keys + 1)
    out = [jax.ShapeDtypeStruct((rows, queries.shape[1]), BF16)]
    stat = pltpu.VMEM((kv_heads, group * rows, 128), F32)
    scratch = [
        pltpu.VMEM((kv_heads, group * rows, HEAD_DIM), BF16),
        pltpu.VMEM((blocks, kv_heads, group * rows, keys), F32),
        stat,
        stat,
        stat,
    ]
    near = (queries, kv)
    if not later:
        out.append(jax.ShapeDtypeStruct((2, total, width), BF16))
        scratch.insert(0, pltpu.SMEM((page_table.shape[0],), jnp.int32))
        near = (queries, *got)
    return one_step(
        functools.partial(attention_kernel, page_len, later),
        "attention",
        out,
        (Far(doc_lengths, pltpu.SMEM), Far(page_table, pltpu.SMEM)),
        near,
        scratch=scratch,
        cost=((0 if later else 1280) * 1280 * group * rows * 128, 0 if later else 4 << 20, 0),
        room=5 * MIB + 4 * kv_heads * group * rows * keys * blocks,
    )


def fetch_kernel(pieces, *refs):
    *given, sem = refs
    given = given[1:]
    count = len(given) // 2
    copies = []
    for k in range(count):
        depth = given[k].shape[0] // pieces
        for i in range(pieces):
            here = slice(i * depth, (i + 1) * depth)
            copies.append(
                pltpu.make_async_copy(
                    given[k].at[here], given[count + k].at[here], sem.at[k * pieces + i]
                )
            )
    for c in copies:
        c.start()
    for c in copies:
        c.wait()


def fetch(after, *weights):
    return pl.pallas_call(
        functools.partial(fetch_kernel, 4),
        out_shape=tuple(jax.ShapeDtypeStruct(w.shape, w.dtype) for w in weights),
        in_specs=[ANY_SPEC] + [HBM_SPEC] * len(weights),
        out_specs=(VMEM_SPEC,) * len(weights),
        scratch_shapes=[pltpu.SemaphoreType.DMA((4 * len(weights),))],
        compiler_params=pltpu.CompilerParams(vmem_limit_bytes=1 * MIB),
        cost_estimate=pl.CostEstimate(
            flops=0, bytes_accessed=2 * sum(w.size for w in weights), transcendentals=0
        ),
        name="fetch",
    )(after, *(in_hbm(w) for w in weights))


def project_kernel(start, tile, side, att_ref, mix_ref, wa_ref, wm_ref, *out):
    part = out[0].shape[0]
    mix = mix_ref[2 * part * side : 2 * part * (side + 1), :]
    for send_ref, keep_ref in zip(out[::2], out[1::2]):
        width = send_ref.shape[1]
        for j in range(0, width, tile):
            here, there = slice(j, j + tile), slice(start + j, start + j + tile)
            total = nn(att_ref[...], wa_ref[:, there]) + nn(mix, wm_ref[:, there])
            send_ref[:, here] = total[:part].astype(BF16)
            keep_ref[:, here] = total[part:]
        start += width


def project(side, att, mix, wa, wm, start, widths, tile):
    rows, depth = att.shape
    width = sum(widths)
    out_shape = []
    for w in widths:
        out_shape.append(jax.ShapeDtypeStruct((rows // 2, w), BF16))
        out_shape.append(jax.ShapeDtypeStruct((rows // 2, w), F32))
    return pl.pallas_call(
        functools.partial(project_kernel, start, tile, side),
        out_shape=tuple(out_shape),
        in_specs=[VMEM_SPEC] * 4,
        out_specs=(VMEM_SPEC,) * len(out_shape),
        compiler_params=pltpu.CompilerParams(vmem_limit_bytes=4 * MIB),
        cost_estimate=pl.CostEstimate(
            flops=(1 - side) * 4 * rows * depth * width,
            bytes_accessed=(1 - side) * 6 * rows * width,
            transcendentals=0,
        ),
        name="project",
    )(att, mix, wa, wm)


def pack_kernel(key_ref, value_ref, out_ref, sem):
    copies = [
        pltpu.make_async_copy(ref, out_ref.at[i], sem.at[i])
        for i, ref in enumerate((key_ref, value_ref))
    ]
    for c in copies:
        c.start()
    for c in copies:
        c.wait()


def pack(keys, values):
    return pl.pallas_call(
        pack_kernel,
        out_shape=jax.ShapeDtypeStruct((2,) + keys.shape, keys.dtype),
        in_specs=[HBM_SPEC] * 2,
        out_specs=VMEM_SPEC,
        scratch_shapes=[pltpu.SemaphoreType.DMA((2,))],
        compiler_params=pltpu.CompilerParams(vmem_limit_bytes=1 * MIB),
        cost_estimate=pl.CostEstimate(flops=0, bytes_accessed=0, transcendentals=0),
        name="pack",
    )(in_hbm(keys), in_hbm(values))


def assemble_kernel(keep_ref, near_ref, *refs):
    *last, out_ref, held, sem = refs
    at, copies = 0, []
    for ref in last:
        here = slice(at, at + ref.shape[1])
        total = keep_ref[:, here] + near_ref[:, here].astype(F32) + ref[...].astype(F32)
        held[:, here] = total.astype(BF16)
        copies.append(
            pltpu.make_async_copy(held.at[:, here], out_ref.at[:, here], sem.at[len(copies)])
        )
        copies[-1].start()
        at += ref.shape[1]
    for c in copies:
        c.wait()


def assemble(keep, near, last):
    return pl.pallas_call(
        assemble_kernel,
        out_shape=jax.ShapeDtypeStruct(keep.shape, BF16),
        in_specs=[VMEM_SPEC] * (2 + len(last)),
        out_specs=HBM_SPEC,
        scratch_shapes=[pltpu.VMEM(keep.shape, BF16), pltpu.SemaphoreType.DMA((len(last),))],
        compiler_params=pltpu.CompilerParams(vmem_limit_bytes=2 * MIB),
        cost_estimate=pl.CostEstimate(flops=0, bytes_accessed=0, transcendentals=0),
        name="assemble",
    )(keep, near, *last)


def shards(
    n_ctx,
    n_tp,
    queries,
    key_pages,
    value_pages,
    mixer_input,
    state_write,
    state_read,
    log_decay,
    skip_gain,
    doc_lengths,
    page_table,
    attention_weight,
    mixer_weight,
):
    tok_rows = queries.shape[0]
    page_len = key_pages.shape[1]
    chips = n_ctx // 2

    def between_chips(a, j):
        return lax.ppermute(a, "ctx", [(i, i ^ (2 * j)) for i in range(n_ctx)])

    def other_core(a):
        return lax.ppermute(a, "ctx", [(i, i ^ 1) for i in range(n_ctx)])

    width = key_pages.shape[2]
    kv = pack(key_pages.reshape(-1, width), value_pages.reshape(-1, width))
    kv, mixer_input = lax.optimization_barrier((kv, mixer_input))
    far = [kv] + [between_chips(kv, j) for j in range(1, chips)]

    base, st, eg = mixer_local(
        doc_lengths, skip_gain, mixer_input, state_write, state_read, log_decay
    )
    low, high = other_core(st[0]), other_core(st[1])
    chip_state = compose(st, low, high)
    near_weight, far_weight, near_queries, near_read = fetch(
        st, attention_weight, mixer_weight, queries, state_read
    )
    far_states = [between_chips(chip_state, j) for j in range(1, chips)]

    far[1:], near_queries, _ = lax.optimization_barrier((far[1:], near_queries, chip_state))
    far[-1], *far_states = lax.optimization_barrier((far[-1], *far_states))
    got = []
    for a in far:
        got += [a, other_core(a)]
    place = (page_len, doc_lengths, page_table, near_queries, width // HEAD_DIM)
    att, kv = attention(*place, got)
    got_states = []
    for a in far_states:
        got_states += [a, other_core(a)]
    mix = finish(base, near_read, eg, low, high, got_states)

    part = tok_rows // n_tp
    columns = attention_weight.shape[1]
    widths = [share * columns // 8 for share in SHARES]
    weights = (near_weight, far_weight)

    def neighbour(a):
        return lax.ppermute(a, "tp", [(i, i ^ 1) for i in range(n_tp)])

    def across(a):
        return lax.ppermute(a, "tp", [(i, i ^ 2) for i in range(n_tp)])

    sums = list(project(0, att, mix, *weights, 0, widths[:1], 256))
    att, sums[0] = lax.optimization_barrier((att, sums[0]))
    sums += project(0, att, mix, *weights, widths[0], widths[1:], 256)
    kv, sums[2] = lax.optimization_barrier((kv, sums[2]))
    near_other = [neighbour(a) for a in sums[::2]]
    last, order = [], None
    for k, keep in enumerate(sums[1::2]):
        if order is not None:
            near_other[k], order = lax.optimization_barrier((near_other[k], order))
        if k == 2:
            near_other[k], last[0] = lax.optimization_barrier((near_other[k], last[0]))
        if k == 2:
            near_other[k], last[1] = lax.optimization_barrier((near_other[k], last[1]))
        order = (keep + near_other[k].astype(F32)).astype(BF16)
        if k == 0:
            kv, order = lax.optimization_barrier((kv, order))
        last.append(across(order))
    (later,) = attention(*place, kv=kv)
    send_own, keep_own = project(1, later, mix, *weights, 0, (columns,), 256)
    near_own = neighbour(send_own)
    return assemble(keep_own, near_own, last)


def solution(mesh):
    placed = (
        P("ctx", "tp"),
        P("ctx", None, "tp"),
        P("ctx", None, "tp"),
        P("ctx", "tp"),
        P("ctx", "tp"),
        P("ctx", "tp"),
        P("tp", "ctx"),
        P("tp"),
        P(),
        P(),
        P("tp", None),
        P("tp", None),
    )
    return jax.shard_map(
        functools.partial(shards, mesh.shape["ctx"], mesh.shape["tp"]),
        mesh=mesh,
        in_specs=placed,
        out_specs=P(("ctx", "tp"), None),
        check_vma=False,
    )
```

```python
import functools

import jax
import jax.numpy as jnp
from jax import lax
from jax.experimental import pallas as pl
from jax.experimental.pallas import tpu as pltpu
from jax.sharding import PartitionSpec as P

HEAD_DIM = 128
SSM_HEAD_DIM = 128
STATE = 128
LOG2E = 1.4426950408889634
LOW = -1e30
SHARES = (2, 3, 3)
F32 = jnp.float32
BF16 = jnp.bfloat16

MIB = 1 << 20
VMEM_SPEC = pl.BlockSpec(memory_space=pltpu.VMEM)
ANY_SPEC = pl.BlockSpec(memory_space=pl.ANY)
HBM_SPEC = pl.BlockSpec(memory_space=pltpu.HBM)


def in_hbm(a):
    return pltpu.with_memory_space_constraint(a, pltpu.HBM)


class Far:
    def __init__(self, array, space=pltpu.VMEM, lanes=None):
        self.array, self.lanes = array, lanes
        shape = array.shape if lanes is None else (array.shape[0], lanes.stop - lanes.start)
        self.scratch = space(shape, array.dtype)


def one_step(kernel, name, out_shape, far, near, scratch=(), cost=(0, 0, 0), room=6 * MIB, specs=None):
    flops, moved, exps = cost

    def body(*refs):
        given, refs = refs[: len(far)], refs[len(far) :]
        rest, held, sem = refs[: -len(far) - 1], refs[-len(far) - 1 : -1], refs[-1]
        copies = []
        for i, (f, src, dst) in enumerate(zip(far, given, held)):
            src = src if f.lanes is None else src.at[:, f.lanes]
            copies.append(pltpu.make_async_copy(src, dst, sem.at[i]))
        for c in copies:
            c.start()
        for c in copies:
            c.wait()
        kernel(*held, *rest)

    return pl.pallas_call(
        body,
        out_shape=tuple(out_shape),
        in_specs=[HBM_SPEC] * len(far) + (specs or [VMEM_SPEC] * len(near)),
        out_specs=(VMEM_SPEC,) * len(out_shape),
        scratch_shapes=[
            *scratch,
            *(f.scratch for f in far),
            pltpu.SemaphoreType.DMA((max(len(far), 1),)),
        ],
        compiler_params=pltpu.CompilerParams(vmem_limit_bytes=room),
        cost_estimate=pl.CostEstimate(flops=flops, bytes_accessed=moved, transcendentals=exps),
        name=name,
    )(*(in_hbm(f.array) for f in far), *near)


def doc_ends_of(len_ref):
    ends, total = [], 0
    for i in range(len_ref.shape[0]):
        total = total + len_ref[i]
        ends.append(total)
    return ends


def doc_start(pos, ends):
    start = jnp.zeros_like(pos)
    for end in ends:
        start = jnp.where(pos >= end, end, start)
    return start


def row_slot(part, z):
    return 3 - (part ^ z)


def nt(a, b):
    return lax.dot_general(a, b, (((1,), (1,)), ((), ())), preferred_element_type=F32)


def nn(a, b):
    return lax.dot_general(a, b, (((1,), (0,)), ((), ())), preferred_element_type=F32)


def mixer_kernel(len_ref, skip_ref, x_ref, w_ref, r_ref, ld_ref, base_ref, st_ref, eg_ref):
    me = lax.axis_index("ctx")
    heads, rows = ld_ref.shape
    groups = w_ref.shape[1] // STATE
    per_group = heads // groups
    half = heads // 2
    first = me * rows
    ends = doc_ends_of(len_ref)
    ds = ld_ref[...]
    lane = lax.broadcasted_iota(jnp.int32, ds.shape, 1)
    shift = 1
    while shift < rows:
        ds = ds + jnp.where(lane >= shift, pltpu.roll(ds, shift, 1), 0.0)
        shift *= 2
    col = ds.T
    t_pos = first + lax.broadcasted_iota(jnp.int32, (rows, 1), 0)
    t_start = doc_start(t_pos, ends)
    s_pos = first + lax.broadcasted_iota(jnp.int32, (1, rows), 1)
    last = first + rows - 1
    last_start = doc_start(jnp.full((1, 1), last, jnp.int32), ends)
    visible = (s_pos <= t_pos) & (s_pos >= t_start)
    bias = jnp.where(visible, 0.0, LOW)
    eg_ref[...] = jnp.where(t_start < first, jnp.exp(col), 0.0)
    total = ds[:, rows - 1 : rows]
    end_weight = jnp.where(s_pos >= last_start, jnp.exp(total - ds), 0.0)
    gain = jnp.where(last_start < first, jnp.exp(total), 0.0)
    gain = jnp.broadcast_to(gain, (heads, SSM_HEAD_DIM)).astype(BF16)
    pad = jnp.zeros((st_ref.shape[1] - half * STATE - half, SSM_HEAD_DIM), BF16)
    for c in range(2):
        st_ref[c, half * STATE :, :] = jnp.concatenate(
            [gain[c * half : (c + 1) * half].astype(F32), pad.astype(F32)], axis=0
        ).astype(BF16)
    for g in range(groups):
        cols = slice(g * STATE, (g + 1) * STATE)
        write, read = w_ref[:, cols], r_ref[:, cols]
        inner = nt(read, write)
        write_t = write.astype(F32).T
        for h in range(g * per_group, (g + 1) * per_group):
            hc = slice(h * SSM_HEAD_DIM, (h + 1) * SSM_HEAD_DIM)
            x = x_ref[:, hc]
            decay = jnp.exp((col[:, h : h + 1] - ds[h : h + 1, :]) + bias)
            mixing = (decay * inner).astype(BF16)
            base_ref[:, hc] = nn(mixing, x) + skip_ref[h] * x.astype(F32)
            end_write = (write_t * end_weight[h : h + 1, :]).astype(BF16)
            c, i = divmod(h, half)
            st_ref[c, i * STATE : (i + 1) * STATE, :] = nn(end_write, x).astype(BF16)


def mixer_local(doc_lengths, skip_gain, x, w, r, ld):
    heads, rows = ld.shape
    half = heads // 2
    return one_step(
        mixer_kernel,
        "mixer_local",
        (
            jax.ShapeDtypeStruct(x.shape, F32),
            jax.ShapeDtypeStruct((2, half * STATE + 16, SSM_HEAD_DIM), BF16),
            jax.ShapeDtypeStruct((rows, heads), F32),
        ),
        (Far(doc_lengths, pltpu.SMEM), Far(skip_gain, pltpu.SMEM), Far(x), Far(w), Far(r), Far(ld)),
        (),
    )


def compose_kernel(mine_ref, other_ref, out_ref):
    core = lax.axis_index("ctx") & 1
    state_rows = out_ref.shape[0] - 16
    half = state_rows // STATE
    a, b = mine_ref[core].astype(F32), other_ref[core].astype(F32)
    first = jnp.where(core == 0, a, b)
    second = jnp.where(core == 0, b, a)
    for i in range(half):
        rows = slice(i * STATE, (i + 1) * STATE)
        gain = second[state_rows + i : state_rows + i + 1]
        out_ref[rows, :] = (gain * first[rows] + second[rows]).astype(BF16)
    out_ref[state_rows:, :] = (first[state_rows:] * second[state_rows:]).astype(BF16)


def compose(mine, other):
    return pl.pallas_call(
        compose_kernel,
        out_shape=jax.ShapeDtypeStruct(mine.shape[1:], BF16),
        in_specs=[VMEM_SPEC] * 2,
        out_specs=VMEM_SPEC,
        compiler_params=pltpu.CompilerParams(vmem_limit_bytes=4 * MIB),
        cost_estimate=pl.CostEstimate(flops=0, bytes_accessed=0, transcendentals=0),
        name="compose",
    )(mine, other)


def finish_kernel(r_ref, base_ref, eg_ref, st_ref, *refs):
    *got, out_ref, held, carry = refs
    me = lax.axis_index("ctx")
    core, chip = me & 1, me // 2
    z = lax.axis_index("tp")
    rows = base_ref.shape[0]
    part = rows // 4
    state_rows = st_ref.shape[1] - 16
    half = state_rows // STATE
    groups = r_ref.shape[1] // STATE
    heads = 2 * half
    per_group = heads // groups
    for j in range(1, held.shape[0]):
        held[chip ^ j, core] = got[2 * j - 2][...]
        held[chip ^ j, core ^ 1] = got[2 * j - 1][...]
    carry[...] = jnp.zeros_like(carry)

    def where(h):
        c, i = divmod(h, half)
        return c, slice(i * STATE, (i + 1) * STATE), slice(state_rows + i, state_rows + i + 1)

    def one(k, _):
        for h in range(heads):
            c, hs, gs = where(h)
            carry[h] = held[k, c, gs, :].astype(F32) * carry[h] + held[k, c, hs, :].astype(F32)
        return 0

    lax.fori_loop(0, chip, one, 0)

    @pl.when(core == 1)
    def _():
        for h in range(heads):
            c, hs, gs = where(h)
            carry[h] = st_ref[c, gs, :].astype(F32) * carry[h] + st_ref[c, hs, :].astype(F32)

    for h in range(heads):
        hc = slice(h * SSM_HEAD_DIM, (h + 1) * SSM_HEAD_DIM)
        g = h // per_group
        inter = nn(r_ref[:, g * STATE : (g + 1) * STATE], carry[h].astype(BF16))
        res = (base_ref[:, hc] + eg_ref[:, h : h + 1] * inter).astype(BF16)
        for q in range(4):
            at = pl.multiple_of(row_slot(q, z) * part, part)
            out_ref[pl.ds(at, part), hc] = res[q * part : (q + 1) * part]


def finish(base, r, eg, st_other, got):
    chips = len(got) // 2 + 1
    heads = base.shape[1] // SSM_HEAD_DIM
    return one_step(
        finish_kernel,
        "finish",
        (jax.ShapeDtypeStruct(base.shape, BF16),),
        (),
        (r, base, eg, st_other, *got),
        scratch=[
            pltpu.VMEM((chips, 2) + got[0].shape, BF16),
            pltpu.VMEM((heads, STATE, SSM_HEAD_DIM), F32),
        ],
        room=(4 + chips) * MIB,
    )[0]


def attention_kernel(page_len, later, len_ref, table_ref, q_ref, *refs):
    if later:
        kv, out_ref, qs, sc, mx, ls, acc = refs
    else:
        *got, out_ref, kv, inv, qs, sc, mx, ls, acc = refs
    me = lax.axis_index("ctx")
    z = lax.axis_index("tp")
    keys = q_ref.shape[0]
    rows = keys // 2
    part = rows // 2
    kv_heads = kv.shape[2] // HEAD_DIM
    group = q_ref.shape[1] // HEAD_DIM // kv_heads
    stacked = group * rows
    ends = doc_ends_of(len_ref)
    start0 = 0
    for end in ends:
        start0 = jnp.where(me * keys >= end, end, start0)
    low_block = start0 // keys
    side = z // 2 if later else 1 - z // 2

    if not later:

        def invert(l, _):
            inv[table_ref[l]] = l
            return 0

        lax.fori_loop(0, table_ref.shape[0], invert, 0, unroll=8)
        for j, ref in enumerate(got):
            pages = ref.shape[1] // page_len
            for slot in range(pages):
                page = inv[(me ^ j) * pages + slot]
                there = pl.ds(pl.multiple_of(page * page_len, page_len), page_len)
                here = slice(slot * page_len, (slot + 1) * page_len)
                for i in range(2):
                    kv[i, there, :] = ref[i, here, :]

    here = pl.ds(pl.multiple_of(side * rows, rows), rows)
    for h in range(kv_heads * group):
        g, i = divmod(h, group)
        qs[g, i * rows : (i + 1) * rows, :] = q_ref[here, h * HEAD_DIM : (h + 1) * HEAD_DIM]
    row = lax.rem(lax.broadcasted_iota(jnp.int32, (min(stacked, 256), 1), 0), rows)
    t_pos = me * keys + side * rows + row
    t_start = doc_start(t_pos, ends)
    scale = LOG2E * HEAD_DIM ** (-0.5)

    def lanes(g):
        return slice(g * HEAD_DIM, (g + 1) * HEAD_DIM)

    unit = min(stacked, 256)
    units = [(g, slice(r, r + unit)) for g in range(kv_heads) for r in range(0, stacked, unit)]

    def scores(block, own):
        at = pl.ds(pl.multiple_of(block * keys, keys), keys)
        u_pos = block * keys + lax.broadcasted_iota(jnp.int32, (1, keys), 1)
        shown = u_pos >= t_start
        if own:
            shown = shown & (u_pos <= t_pos)
        for g, r in units:
            s = nt(qs[g, r, :], kv[0, at, lanes(g)])
            s = jnp.where(shown, s * scale, LOW)
            sc[block - low_block, g, r, :] = s
            top = s[:, :128]
            for k in range(128, keys, 128):
                top = jnp.maximum(top, s[:, k : k + 128])
            mx[g, r, :] = top if own else jnp.maximum(mx[g, r, :], top)

    scores(me, True)

    def earlier(block, _):
        scores(block, False)
        return 0

    lax.fori_loop(low_block, me, earlier, 0)
    for g in range(kv_heads):
        mx[g] = jnp.broadcast_to(jnp.max(mx[g], axis=1, keepdims=True), (stacked, 128))

    def weigh(block, own):
        at = pl.ds(pl.multiple_of(block * keys, keys), keys)
        for g, r in units:
            m = mx[g, r, :]
            total, pieces = None, []
            for k in range(0, keys, 128):
                w = jnp.exp2(sc[block - low_block, g, r, k : k + 128] - m)
                total = w if total is None else total + w
                pieces.append(w.astype(BF16))
            term = nn(jnp.concatenate(pieces, axis=1), kv[1, at, lanes(g)])
            ls[g, r, :] = total if own else ls[g, r, :] + total
            acc[g, r, :] = term if own else acc[g, r, :] + term

    weigh(me, True)

    def weigh_earlier(block, _):
        weigh(block, False)
        return 0

    lax.fori_loop(low_block, me, weigh_earlier, 0)
    for g in range(kv_heads):
        inverse = 1.0 / jnp.sum(ls[g], axis=1, keepdims=True)
        res = (acc[g] * inverse).astype(BF16)
        for i in range(group):
            h = g * group + i
            for q in range(2):
                slot = row_slot(2 * side + q, z) - (2 if later else 0)
                at = pl.multiple_of(slot * part, part)
                src = i * rows + q * part
                out_ref[pl.ds(at, part), h * HEAD_DIM : (h + 1) * HEAD_DIM] = res[src : src + part]


def attention(page_len, doc_lengths, page_table, queries, kv_heads, got=(), kv=None):
    later = kv is not None
    keys = queries.shape[0]
    rows = keys // 2
    group = queries.shape[1] // HEAD_DIM // kv_heads
    total = kv.shape[1] if later else len(got) * keys
    width = kv_heads * HEAD_DIM
    blocks = min(total // keys, total // 2 // keys + 1)
    out = [jax.ShapeDtypeStruct((rows, queries.shape[1]), BF16)]
    stat = pltpu.VMEM((kv_heads, group * rows, 128), F32)
    scratch = [
        pltpu.VMEM((kv_heads, group * rows, HEAD_DIM), BF16),
        pltpu.VMEM((blocks, kv_heads, group * rows, keys), F32),
        stat,
        stat,
        stat,
    ]
    near = (queries, kv)
    if not later:
        out.append(jax.ShapeDtypeStruct((2, total, width), BF16))
        scratch.insert(0, pltpu.SMEM((page_table.shape[0],), jnp.int32))
        near = (queries, *got)
    return one_step(
        functools.partial(attention_kernel, page_len, later),
        "attention",
        out,
        (Far(doc_lengths, pltpu.SMEM), Far(page_table, pltpu.SMEM)),
        near,
        scratch=scratch,
        cost=((0 if later else 1280) * 1280 * group * rows * 128, 0 if later else 4 << 20, 0),
        room=5 * MIB + 4 * kv_heads * group * rows * keys * blocks,
    )


def fetch_kernel(pieces, *refs):
    *given, sem = refs
    given = given[1:]
    count = len(given) // 2
    copies = []
    for k in range(count):
        depth = given[k].shape[0] // pieces
        for i in range(pieces):
            here = slice(i * depth, (i + 1) * depth)
            copies.append(
                pltpu.make_async_copy(
                    given[k].at[here], given[count + k].at[here], sem.at[k * pieces + i]
                )
            )
    for c in copies:
        c.start()
    for c in copies:
        c.wait()


def fetch(after, *weights):
    return pl.pallas_call(
        functools.partial(fetch_kernel, 4),
        out_shape=tuple(jax.ShapeDtypeStruct(w.shape, w.dtype) for w in weights),
        in_specs=[ANY_SPEC] + [HBM_SPEC] * len(weights),
        out_specs=(VMEM_SPEC,) * len(weights),
        scratch_shapes=[pltpu.SemaphoreType.DMA((4 * len(weights),))],
        compiler_params=pltpu.CompilerParams(vmem_limit_bytes=1 * MIB),
        cost_estimate=pl.CostEstimate(
            flops=0, bytes_accessed=2 * sum(w.size for w in weights), transcendentals=0
        ),
        name="fetch",
    )(after, *(in_hbm(w) for w in weights))


def project_kernel(start, tile, side, att_ref, mix_ref, wa_ref, wm_ref, *out):
    part = out[0].shape[0]
    mix = mix_ref[2 * part * side : 2 * part * (side + 1), :]
    for send_ref, keep_ref in zip(out[::2], out[1::2]):
        width = send_ref.shape[1]
        for j in range(0, width, tile):
            here, there = slice(j, j + tile), slice(start + j, start + j + tile)
            total = nn(att_ref[...], wa_ref[:, there]) + nn(mix, wm_ref[:, there])
            send_ref[:, here] = total[:part].astype(BF16)
            keep_ref[:, here] = total[part:]
        start += width


def project(side, att, mix, wa, wm, start, widths, tile):
    rows, depth = att.shape
    width = sum(widths)
    out_shape = []
    for w in widths:
        out_shape.append(jax.ShapeDtypeStruct((rows // 2, w), BF16))
        out_shape.append(jax.ShapeDtypeStruct((rows // 2, w), F32))
    return pl.pallas_call(
        functools.partial(project_kernel, start, tile, side),
        out_shape=tuple(out_shape),
        in_specs=[VMEM_SPEC] * 4,
        out_specs=(VMEM_SPEC,) * len(out_shape),
        compiler_params=pltpu.CompilerParams(vmem_limit_bytes=4 * MIB),
        cost_estimate=pl.CostEstimate(
            flops=(1 - side) * 4 * rows * depth * width,
            bytes_accessed=(1 - side) * 6 * rows * width,
            transcendentals=0,
        ),
        name="project",
    )(att, mix, wa, wm)


def pack_kernel(key_ref, value_ref, out_ref, sem):
    copies = [
        pltpu.make_async_copy(ref, out_ref.at[i], sem.at[i])
        for i, ref in enumerate((key_ref, value_ref))
    ]
    for c in copies:
        c.start()
    for c in copies:
        c.wait()


def pack(keys, values):
    return pl.pallas_call(
        pack_kernel,
        out_shape=jax.ShapeDtypeStruct((2,) + keys.shape, keys.dtype),
        in_specs=[HBM_SPEC] * 2,
        out_specs=VMEM_SPEC,
        scratch_shapes=[pltpu.SemaphoreType.DMA((2,))],
        compiler_params=pltpu.CompilerParams(vmem_limit_bytes=1 * MIB),
        cost_estimate=pl.CostEstimate(flops=0, bytes_accessed=0, transcendentals=0),
        name="pack",
    )(in_hbm(keys), in_hbm(values))


def assemble_kernel(keep_ref, near_ref, *refs):
    *last, out_ref, held, sem = refs
    at, copies = 0, []
    for ref in last:
        here = slice(at, at + ref.shape[1])
        total = keep_ref[:, here] + near_ref[:, here].astype(F32) + ref[...].astype(F32)
        held[:, here] = total.astype(BF16)
        copies.append(
            pltpu.make_async_copy(held.at[:, here], out_ref.at[:, here], sem.at[len(copies)])
        )
        copies[-1].start()
        at += ref.shape[1]
    for c in copies:
        c.wait()


def assemble(keep, near, last):
    return pl.pallas_call(
        assemble_kernel,
        out_shape=jax.ShapeDtypeStruct(keep.shape, BF16),
        in_specs=[VMEM_SPEC] * (2 + len(last)),
        out_specs=HBM_SPEC,
        scratch_shapes=[pltpu.VMEM(keep.shape, BF16), pltpu.SemaphoreType.DMA((len(last),))],
        compiler_params=pltpu.CompilerParams(vmem_limit_bytes=2 * MIB),
        cost_estimate=pl.CostEstimate(flops=0, bytes_accessed=0, transcendentals=0),
        name="assemble",
    )(keep, near, *last)


def shards(
    n_ctx,
    n_tp,
    queries,
    key_pages,
    value_pages,
    mixer_input,
    state_write,
    state_read,
    log_decay,
    skip_gain,
    doc_lengths,
    page_table,
    attention_weight,
    mixer_weight,
):
    tok_rows = queries.shape[0]
    page_len = key_pages.shape[1]
    chips = n_ctx // 2

    def between_chips(a, j):
        return lax.ppermute(a, "ctx", [(i, i ^ (2 * j)) for i in range(n_ctx)])

    def other_core(a):
        return lax.ppermute(a, "ctx", [(i, i ^ 1) for i in range(n_ctx)])

    width = key_pages.shape[2]
    kv = pack(key_pages.reshape(-1, width), value_pages.reshape(-1, width))
    kv, mixer_input = lax.optimization_barrier((kv, mixer_input))
    far = [kv] + [between_chips(kv, j) for j in range(1, chips)]

    base, st, eg = mixer_local(
        doc_lengths, skip_gain, mixer_input, state_write, state_read, log_decay
    )
    st_other = other_core(st)
    chip_state = compose(st, st_other)
    near_weight, far_weight, near_queries, near_read = fetch(
        st, attention_weight, mixer_weight, queries, state_read
    )
    far_states = [between_chips(chip_state, j) for j in range(1, chips)]

    far[1:], near_queries = lax.optimization_barrier((far[1:], near_queries))
    got = []
    for a in far:
        got += [a, other_core(a)]
    place = (page_len, doc_lengths, page_table, near_queries, width // HEAD_DIM)
    att, kv = attention(*place, got)
    *far_states, att = lax.optimization_barrier((*far_states, att))
    got_states = []
    for a in far_states:
        got_states += [a, other_core(a)]
    mix = finish(base, near_read, eg, st_other, got_states)

    part = tok_rows // n_tp
    columns = attention_weight.shape[1]
    widths = [share * columns // 8 for share in SHARES]
    weights = (near_weight, far_weight)

    def neighbour(a):
        return lax.ppermute(a, "tp", [(i, i ^ 1) for i in range(n_tp)])

    def across(a):
        return lax.ppermute(a, "tp", [(i, i ^ 2) for i in range(n_tp)])

    sums = list(project(0, att, mix, *weights, 0, widths[:1], 256))
    att, sums[0] = lax.optimization_barrier((att, sums[0]))
    sums += project(0, att, mix, *weights, widths[0], widths[1:], 256)
    kv, sums[2] = lax.optimization_barrier((kv, sums[2]))
    near_other = [neighbour(a) for a in sums[::2]]
    last, order = [], None
    for k, keep in enumerate(sums[1::2]):
        if order is not None:
            near_other[k], order = lax.optimization_barrier((near_other[k], order))
        if k == 2:
            near_other[k], last[0] = lax.optimization_barrier((near_other[k], last[0]))
        if k == 2:
            near_other[k], last[1] = lax.optimization_barrier((near_other[k], last[1]))
        order = (keep + near_other[k].astype(F32)).astype(BF16)
        if k == 0:
            kv, order = lax.optimization_barrier((kv, order))
        last.append(across(order))
    (later,) = attention(*place, kv=kv)
    send_own, keep_own = project(1, later, mix, *weights, 0, (columns,), 256)
    near_own = neighbour(send_own)
    return assemble(keep_own, near_own, last)


def solution(mesh):
    placed = (
        P("ctx", "tp"),
        P("ctx", None, "tp"),
        P("ctx", None, "tp"),
        P("ctx", "tp"),
        P("ctx", "tp"),
        P("ctx", "tp"),
        P("tp", "ctx"),
        P("tp"),
        P(),
        P(),
        P("tp", None),
        P("tp", None),
    )
    return jax.shard_map(
        functools.partial(shards, mesh.shape["ctx"], mesh.shape["tp"]),
        mesh=mesh,
        in_specs=placed,
        out_specs=P(("ctx", "tp"), None),
        check_vma=False,
    )
```
